128 devices in a mesh: pipe: 2 (over core), dp: 4 (over x), tensor: 16 (over z, y).
Axes of the slice: x: 4, y: 4, z: 4, core: 2. Of those that a mesh axis runs over, the one named last changes fastest.
Arguments:
- embedded: bfloat16 [512, 4096], P('dp', 'pipe'), may hold values from -6 to 6
- rotation_scaled: float32 [4096, 4096], P(('pipe', 'dp'), 'tensor'), as said below
- value_proj: bfloat16 [2, 4096, 1024], P('pipe', 'tensor'), may hold values from -0.09375 to 0.09375
- output_proj: bfloat16 [2, 1024, 4096], P('pipe', None, 'tensor'), may hold values from -0.1875 to 0.1875
- mid_exponent: int32 [2, 1024], P('pipe'), may hold values from -3 to -1
- cotangent: bfloat16 [512, 4096], P('dp', 'tensor'), may hold values from -6 to 6
Outputs:
- rotation_next: float32 [4096, 4096], P(('pipe', 'dp'), 'tensor')
The draws below stay inside these ranges and needn't reach their ends.
Inputs may be any that keep to these rules, and one draw needn't show every extreme that they name: rotation_scaled / sqrt(4096) is orthogonal.
All inputs are finite; a program needn't handle non-finite values.
Results may differ from the reference program's by a relative error of at most 0.017.
Values may be sent and summed in bfloat16 or wider, within the bound.
A program may use at most 64 MiB of HBM per device.

```python
import math
import jax
import jax.numpy as jnp
from jax import lax

D = 4096
K = 1024
MB = 4
TOK_MB = 32
BLOCKS = 2
TOKENS = 512
N_PIPE = 2
N_DP = 4
N_TENSOR = 16


def draw_rotation_scaled(key, part):
    normals = jax.random.normal(jax.random.fold_in(key, 17), (D, D), jnp.float32)
    orthog, triangle = jnp.linalg.qr(normals)
    return (orthog * math.sqrt(D)).astype(jnp.float32)


def place_ends(result, stream_key, least, top_value):
    longest = result.shape.index(max(result.shape))
    spots = []
    for shift in (0, 1):
        where = [jax.random.randint(jax.random.fold_in(stream_key, axis), (), 0, length) for axis, length in enumerate(result.shape)]
        where[longest] = (where[longest] + shift) % result.shape[longest]
        spots.append(tuple(where))
    return result.at[spots[0]].set(least).at[spots[1]].set(top_value)


def shard_levels(own_key, dims, cuts, least, top_value):
    gain = 1.0
    for axis_at, blocks in cuts:
        steps = jax.random.uniform(jax.random.fold_in(jax.random.fold_in(own_key, 6), axis_at), (blocks,), jnp.float32, least / len(cuts), top_value / len(cuts))
        gain = gain * jnp.repeat(jnp.exp(steps), dims[axis_at] // blocks).reshape((-1,) + (1,) * (len(dims) - 1 - axis_at))
    return gain


def centred(stream_key, shape, spread, bound, shards=(), kind=jnp.bfloat16):
    result = jax.random.normal(stream_key, shape, jnp.float32) * spread
    if len(shards) > 0:
        result = shard_levels(stream_key, shape, shards, -0.22, 0.18) * result
    return jnp.clip(result, min=-bound, max=bound).astype(kind)


def setup_inputs(seed: int = 0) -> dict:
    arg_keys = jax.random.split(jax.random.key(seed), 7)
    embedded = centred(arg_keys[0], (TOKENS, D), 1.0, 6.0, ((0, 4), (1, 2)))
    rotation_scaled = draw_rotation_scaled(jax.random.fold_in(arg_keys[6], 71), 0)
    value_proj = centred(arg_keys[2], (BLOCKS, D, K), D ** -0.5, 0.09375, ((0, 2), (1, 16)))
    output_proj = centred(arg_keys[3], (BLOCKS, K, D), K ** -0.5, 0.1875, ((0, 2), (2, 16)))
    mid_exponent = place_ends(jax.random.randint(arg_keys[4], (BLOCKS, K), -3, 0), jax.random.fold_in(arg_keys[4], 1), -3, -1).astype(jnp.int32)
    cotangent = centred(arg_keys[5], (TOKENS, D), 1.0, 6.0, ((0, 4), (1, 16)))
    return {"embedded": embedded, "rotation_scaled": rotation_scaled, "value_proj": value_proj, "output_proj": output_proj, "mid_exponent": mid_exponent, "cotangent": cotangent}


def block_sum(left_side, right_side, parts):
    block_width = left_side.shape[1] // parts
    accumulated = jnp.zeros((left_side.shape[0], right_side.shape[1]), jnp.float32)
    for position in range(parts):
        partial_value = jnp.dot(left_side[:, position * block_width:(position + 1) * block_width].astype(jnp.float32), right_side[position * block_width:(position + 1) * block_width].astype(jnp.float32), preferred_element_type=jnp.float32)
        accumulated = accumulated + lax.optimization_barrier(partial_value.astype(jnp.bfloat16)).astype(jnp.float32)
    return accumulated

def reference(embedded, rotation_scaled, value_proj, output_proj, mid_exponent, cotangent):
    rotation = rotation_scaled / math.sqrt(D)
    rot_low = rotation.astype(jnp.bfloat16)
    start_field = block_sum(embedded, rot_low, N_PIPE)
    hidden = start_field.astype(jnp.bfloat16)
    saved = []
    for section_index in range(N_PIPE):
        weight_in = value_proj[section_index]
        weight_out = output_proj[section_index]
        bounds = jnp.exp2(mid_exponent[section_index].astype(jnp.float32))
        hidden_f = hidden.astype(jnp.float32)
        inv_rms = lax.rsqrt(lax.optimization_barrier(jnp.mean(hidden_f * hidden_f, axis=1, keepdims=True)) + 1e-05)
        summed = jnp.dot(hidden.astype(jnp.float32), weight_in.astype(jnp.float32), preferred_element_type=jnp.float32)
        gated_rows = inv_rms * summed
        clipped = jnp.clip(gated_rows, -8.0 * bounds, 7.0 * bounds).astype(jnp.bfloat16)
        branch_out = jnp.dot(clipped.astype(jnp.float32), weight_out.astype(jnp.float32), preferred_element_type=jnp.float32)
        saved.append((hidden, summed, inv_rms, bounds))
        hidden = (hidden_f + branch_out).astype(jnp.bfloat16)
    incoming = cotangent
    for section_index in range(N_PIPE - 1, -1, -1):
        weight_in = value_proj[section_index]
        weight_out = output_proj[section_index]
        hidden, summed, inv_rms, bounds = saved[section_index]
        back_sum = jnp.dot(incoming.astype(jnp.float32), weight_out.T.astype(jnp.float32), preferred_element_type=jnp.float32)
        gated_rows = inv_rms * summed
        inside = (gated_rows >= -8.0 * bounds) & (gated_rows <= 7.0 * bounds)
        scaled_grad = (inv_rms * jnp.where(inside, back_sum, 0.0)).astype(jnp.bfloat16)
        linear = jnp.dot(scaled_grad.astype(jnp.float32), weight_in.T.astype(jnp.float32), preferred_element_type=jnp.float32)
        statistic = lax.optimization_barrier(jnp.sum(scaled_grad.astype(jnp.float32) * summed, axis=1, keepdims=True))
        grad_field = incoming.astype(jnp.float32) + linear - inv_rms * inv_rms / D * statistic * hidden.astype(jnp.float32)
        incoming = grad_field.astype(jnp.bfloat16)
    embed_grad = block_sum(incoming, rot_low.T, N_TENSOR).astype(jnp.bfloat16)
    turned = block_sum(embed_grad, rot_low, N_PIPE)
    group_rows = MB * TOK_MB
    embed_groups = embedded.reshape(N_DP, group_rows, D)
    grad_groups = embed_grad.reshape(N_DP, group_rows, D)
    left_rows = jnp.concatenate([embed_groups, grad_groups], axis=1).reshape(2 * TOKENS, D)
    right_rows = jnp.concatenate([grad_groups, -embed_groups], axis=1).reshape(2 * TOKENS, D)
    first_dirs = (2.0 * jnp.concatenate([turned.reshape(N_DP, group_rows, D), -start_field.reshape(N_DP, group_rows, D)], axis=1)).astype(jnp.bfloat16).reshape(2 * TOKENS, D)
    step_one = jnp.dot(left_rows.T.astype(jnp.float32), first_dirs.astype(jnp.float32), preferred_element_type=jnp.float32)
    step_rate = jnp.sqrt(D / (jnp.sum(step_one * step_one) + 1e-06))
    first_iter = rotation - 0.5 * step_rate * step_one
    iterate = (rotation + first_iter).astype(jnp.bfloat16)
    second_dirs = block_sum(right_rows, iterate, N_PIPE).astype(jnp.bfloat16)
    step_two = jnp.dot(left_rows.T.astype(jnp.float32), second_dirs.astype(jnp.float32), preferred_element_type=jnp.float32)
    return math.sqrt(D) * (rotation - 0.5 * step_rate * step_two)
```

```python
import functools
import math

import jax
import jax.numpy as jnp
from jax import lax
from jax.experimental import pallas as pl
from jax.experimental.pallas import tpu as pltpu
from jax.sharding import PartitionSpec as P

BF = jnp.bfloat16
F32 = jnp.float32
LANES = 128
NT_DIMS = (((1,), (1,)), ((), ()))


def dot(a, b):
    return jnp.dot(a, b, preferred_element_type=F32)


def dot_nt(a, b):
    return lax.dot_general(a, b, NT_DIMS, preferred_element_type=F32)


def kernel(
    nd,
    nt,
    width,
    e_ref,
    r_ref,
    v_ref,
    o_ref,
    m_ref,
    u_ref,
    out_ref,
    rg,
    xpart,
    xrecv,
    xall,
    eall,
    gall,
    v1,
    bnd,
    bnd1,
    dcbuf,
    dc1recv,
    ybuf,
    y0recv,
    y1recv,
    cbuf,
    qbuf,
    dc0recv,
    q0buf,
    vpart,
    vrecv,
    vall,
    msbuf,
    msrecv,
    msall,
    nsbuf,
    nsrecv,
    nstbuf,
    nstrecv,
    tsend,
    trecv,
    xsend,
    xrecv_sem,
    gsend,
    grecv,
    psend,
    precv,
):
    p = lax.axis_index("pipe")
    d = lax.axis_index("dp")
    t = lax.axis_index("tensor")
    tg = u_ref.shape[0]
    half = ybuf.shape[2] - LANES
    own = tg // (nt // 2)
    rows = rg.shape[1]
    group = 2 * nd
    slot = p * nd + d
    my_half = lax.rem(t, 2)
    my_tok = pl.multiple_of((t // 2) * own, own)

    def rcopy(src, dst, ssem, rsem, to):
        return pltpu.make_async_remote_copy(
            src_ref=src,
            dst_ref=dst,
            send_sem=ssem,
            recv_sem=rsem,
            device_id=to,
            device_id_type=pl.DeviceIdType.MESH,
        )

    def loop(n, body):
        def step(k, carry):
            body(k)
            return carry

        lax.fori_loop(1, n, step, 0)

    def plane(k):
        return lax.rem(t + k, nt)

    def plane_back(k):
        return lax.rem(t + nt - k, nt)

    def piece(buf, j):
        return buf.at[lax.rem(j, 2), pl.ds(pl.multiple_of((j // 2) * own, own), own)]

    def rs_copy(buf, recv, ph, k):
        j = plane(k)
        return rcopy(piece(buf, j), recv.at[k], tsend.at[ph, k], trecv.at[ph, k], (p, d, j))

    def rs_start(buf, recv, ph):
        loop(nt, lambda k: rs_copy(buf, recv, ph, k).start())

    def rs_wait(buf, recv, ph):
        loop(nt, lambda k: rs_copy(buf, recv, ph, k).wait_recv())
        total = buf[my_half, pl.ds(my_tok, own)].astype(F32)
        for k in range(1, nt):
            total = total + recv[k].astype(F32)
        return total

    def ag_copy(buf, ph, k, j):
        return rcopy(piece(buf, j), piece(buf, j), tsend.at[ph, k], trecv.at[ph, k], (p, d, plane(k)))

    def ag_start(buf, ph):
        loop(nt, lambda k: ag_copy(buf, ph, k, t).start())

    def ag_wait(buf, ph):
        loop(nt, lambda k: ag_copy(buf, ph, k, plane_back(k)).wait_recv())

    def ring(k):
        return lax.rem(d + k, nd)

    def ring_back(k):
        return lax.rem(d + nd - k, nd)

    partner = (1 - p, d, t)

    bar = pltpu.get_barrier_semaphore()

    def greet(to):
        pl.semaphore_signal(bar, inc=1, device_id=to, device_id_type=pl.DeviceIdType.MESH)

    loop(nt, lambda k: greet((p, d, plane(k))))
    loop(nd, lambda k: greet((p, ring(k), t)))
    loop(nd, lambda k: greet((1 - p, ring(k), t)))
    greet(partner)

    rg[pl.ds(d, 1)] = (r_ref[...] * (1.0 / math.sqrt(width))).astype(BF)[None]
    bnd[...] = jnp.broadcast_to(jnp.exp2(m_ref[...].astype(F32)), bnd.shape)

    pl.semaphore_wait(bar, nt - 1 + 2 * (nd - 1) + 1)

    def r_copy(k, s):
        return rcopy(rg.at[s], rg.at[s], xsend.at[0, k], xrecv_sem.at[0, k], (p, ring(k), t))

    loop(nd, lambda k: r_copy(k, d).start())

    v1_copy = rcopy(v_ref.at[0], v1, psend.at[0], precv.at[0], partner)
    b1_copy = rcopy(bnd, bnd1, psend.at[1], precv.at[1], partner)
    d1_copy = rcopy(dcbuf, dcbuf, psend.at[2], precv.at[2], partner)

    @pl.when(p == 1)
    def _():
        part = dot_nt(u_ref[...], o_ref[0])
        dcbuf[0] = part[:, :half].astype(BF)
        dcbuf[1] = part[:, half:].astype(BF)
        d1_copy.start()
        b1_copy.start()
        v1_copy.start()

    @pl.when(p == 0)
    def _():
        d1_copy.wait_recv()
        rs_start(dcbuf, dc1recv, 0)

    loop(nd, lambda k: r_copy(k, ring_back(k)).wait_recv())
    part = dot(e_ref[...], rg[...].reshape(nd * rows, rg.shape[2])).astype(BF)
    xpart[...] = part
    x_copy = rcopy(xpart, xrecv, psend.at[3], precv.at[3], partner)
    x_copy.start()
    x_copy.wait_recv()
    hid0 = (xpart[...].astype(F32) + xrecv[...].astype(F32)).astype(BF)
    xall[pl.ds(d, 1)] = hid0[None]

    def h_copy(k, s):
        return rcopy(xall.at[s], xall.at[s], xsend.at[1, k], xrecv_sem.at[1, k], (p, ring(k), t))

    def e_copy(k, src, dst):
        cols = pl.ds(pl.multiple_of(src * rows, LANES), rows)
        return rcopy(e_ref.at[:, cols], eall.at[dst], xsend.at[2, k], xrecv_sem.at[2, k], (p, ring(k), t))

    def g_copy(k, to, s):
        return rcopy(gall.at[s], gall.at[s], gsend.at[k], grecv.at[k], to)

    @pl.when(p == 0)
    def _():
        def store_y(y, h):
            hf = h.astype(F32)
            sq = jnp.broadcast_to(jnp.sum(hf * hf, axis=1, keepdims=True), (tg, LANES))
            ybuf[0, :, :half] = y[:, :half]
            ybuf[1, :, :half] = y[:, half:]
            ybuf[0, :, half:] = sq
            ybuf[1, :, half:] = sq

        def pick(b):
            return jnp.where(my_half == 0, b[0:1, :half], b[0:1, half:])

        def norm(total):
            return lax.rsqrt(total[:, half : half + 1] / width + 1e-05)

        def store_q(buf, q, coef):
            hi = coef.astype(BF)
            lo = (coef - hi.astype(F32)).astype(BF)
            lane = lax.broadcasted_iota(jnp.int32, (own, LANES), 1)
            ext = jnp.where(
                lane < LANES // 2,
                jnp.broadcast_to(hi.astype(F32), (own, LANES)),
                jnp.broadcast_to(lo.astype(F32), (own, LANES)),
            )
            buf[my_half, pl.ds(my_tok, own), pl.ds(0, half)] = q
            buf[my_half, pl.ds(my_tok, own), pl.ds(half, LANES)] = ext.astype(BF)

        def load_coef(buf):
            ext = buf[0, :, half:].astype(F32) + buf[1, :, half:].astype(F32)
            return jnp.sum(ext, axis=1, keepdims=True) * (2.0 / LANES)

        def gate(total, dc, inv, bound, buf):
            y = total[:, :half]
            z = inv * y
            inside = (z >= -8.0 * bound) & (z <= 7.0 * bound)
            q = (inv * jnp.where(inside, dc, 0.0)).astype(BF)
            stat = jnp.sum(q.astype(F32) * y, axis=1, keepdims=True)
            store_q(buf, q, inv * inv / width * stat)

        h0 = xall[d]
        store_y(dot(h0, v_ref[0]), h0)
        rs_start(ybuf, y0recv, 1)
        loop(nd, lambda k: h_copy(k, d).start())
        loop(nd, lambda k: e_copy(k, ring(k), d).start())
        eall[pl.ds(d, 1)] = e_ref[:, pl.ds(pl.multiple_of(d * rows, LANES), rows)][None]
        tot0 = rs_wait(ybuf, y0recv, 1)
        inv0 = norm(tot0)
        bound0 = pick(bnd)
        c0 = jnp.clip(inv0 * tot0[:, :half], -8.0 * bound0, 7.0 * bound0).astype(BF)
        cbuf[my_half, pl.ds(my_tok, own)] = c0
        ag_start(cbuf, 2)
        loop(nt, lambda k: rs_copy(ybuf, y0recv, 1, k).wait_send())
        ag_wait(cbuf, 2)
        wo = o_ref[0]
        branch = dot(cbuf[0], wo[:half]) + dot(cbuf[1], wo[half:])
        h1 = (xall[d].astype(F32) + branch).astype(BF)
        v1_copy.wait_recv()
        b1_copy.wait_recv()
        store_y(dot(h1, v1[...]), h1)
        rs_start(ybuf, y1recv, 3)
        loop(nt, lambda k: rs_copy(dcbuf, dc1recv, 0, k).wait_send())
        dc1 = rs_wait(dcbuf, dc1recv, 0)
        tot1 = rs_wait(ybuf, y1recv, 3)
        gate(tot1, dc1, norm(tot1), pick(bnd1), qbuf)
        ag_start(qbuf, 4)
        ag_wait(qbuf, 4)
        w1 = v1[...]
        lin1 = dot_nt(qbuf[0, :, :half], w1[:, :half]) + dot_nt(qbuf[1, :, :half], w1[:, half:])
        u1 = (u_ref[...].astype(F32) + lin1 - load_coef(qbuf) * h1.astype(F32)).astype(BF)
        dpart = dot_nt(u1, o_ref[0])
        dcbuf[0] = dpart[:, :half].astype(BF)
        dcbuf[1] = dpart[:, half:].astype(BF)
        rs_start(dcbuf, dc0recv, 5)
        dc0 = rs_wait(dcbuf, dc0recv, 5)
        gate(tot0, dc0, inv0, bound0, q0buf)
        ag_start(q0buf, 6)
        ag_wait(q0buf, 6)
        w0 = v_ref[0]
        lin0 = dot_nt(q0buf[0, :, :half], w0[:, :half]) + dot_nt(q0buf[1, :, :half], w0[:, half:])
        g0 = (u1.astype(F32) + lin0 - load_coef(q0buf) * xall[d].astype(F32)).astype(BF)
        gall[pl.ds(d, 1)] = g0[None]
        loop(nd, lambda k: g_copy(k, (0, ring(k), t), d).start())
        g_copy(0, partner, d).start()
        loop(nd, lambda k: g_copy(nd + k, (1, ring(k), t), d).start())
        loop(nd, lambda k: g_copy(k, (0, ring(k), t), ring_back(k)).wait_recv())
        loop(nt, lambda k: ag_copy(cbuf, 2, k, t).wait_send())
        loop(nt, lambda k: rs_copy(ybuf, y1recv, 3, k).wait_send())
        loop(nt, lambda k: ag_copy(qbuf, 4, k, t).wait_send())
        loop(nt, lambda k: rs_copy(dcbuf, dc0recv, 5, k).wait_send())
        loop(nt, lambda k: ag_copy(q0buf, 6, k, t).wait_send())
        loop(nd, lambda k: g_copy(k, (0, ring(k), t), d).wait_send())
        g_copy(0, partner, d).wait_send()
        loop(nd, lambda k: g_copy(nd + k, (1, ring(k), t), d).wait_send())

    @pl.when(p == 1)
    def _():
        loop(nd, lambda k: h_copy(k, d).start())
        loop(nd, lambda k: e_copy(k, ring(k), d).start())
        eall[pl.ds(d, 1)] = e_ref[:, pl.ds(pl.multiple_of(d * rows, LANES), rows)][None]
        d1_copy.wait_send()
        b1_copy.wait_send()
        v1_copy.wait_send()
        g_copy(0, partner, d).wait_recv()
        loop(nd, lambda k: g_copy(nd + k, (1, ring(k), t), ring_back(k)).wait_recv())

    tokens = nd * tg
    grad = gall[...].reshape(tokens, gall.shape[2])
    vpart[...] = dot_nt(rg[d], grad).astype(BF)
    vrow = rows // nt

    def vpiece(buf, j):
        return buf.at[pl.ds(pl.multiple_of(j * vrow, vrow), vrow)]

    def vrs(k):
        j = plane(k)
        return rcopy(vpiece(vpart, j), vrecv.at[k], tsend.at[7, k], trecv.at[7, k], (p, d, j))

    def vag(k, j):
        return rcopy(vpiece(vall, j), vpiece(vall, j), tsend.at[8, k], trecv.at[8, k], (p, d, plane(k)))

    loop(nt, lambda k: vrs(k).start())
    loop(nd, lambda k: h_copy(k, ring_back(k)).wait_recv())
    loop(nd, lambda k: e_copy(k, d, ring_back(k)).wait_recv())
    emb = eall[...].reshape(tokens, rows)
    emb_t = emb.T
    front = dot(emb_t, grad)
    loop(nt, lambda k: vrs(k).wait_recv())
    vsum = vpart[pl.ds(pl.multiple_of(t * vrow, vrow), vrow)].astype(F32)
    for k in range(1, nt):
        vsum = vsum + vrecv[k].astype(F32)
    vall[pl.ds(pl.multiple_of(t * vrow, vrow), vrow)] = vsum.astype(BF)
    loop(nt, lambda k: vag(k, t).start())
    loop(nt, lambda k: vag(k, plane_back(k)).wait_recv())
    vt = vall[...]
    hid = xall[...].reshape(tokens, xall.shape[2])
    s0 = 2.0 * (front - dot(vt, hid))
    nsbuf[...] = jnp.broadcast_to(jnp.sum(s0 * s0), nsbuf.shape)
    s0b = s0.astype(BF)
    msbuf[pl.ds(0, nd)] = dot(vt.T, s0b).astype(BF).reshape(nd, tg, -1)
    msbuf[pl.ds(nd, nd)] = (-dot(emb, s0b)).astype(BF).reshape(nd, tg, -1)

    def cell(j):
        return (j // nd, lax.rem(j, nd), t)

    def fwd(k):
        return lax.rem(slot + k, group)

    def back(k):
        return lax.rem(slot + group - k, group)

    def ns_copy(k):
        return rcopy(nsbuf, nsrecv.at[k], gsend.at[group + k], grecv.at[group + k], cell(fwd(k)))

    def ms_copy(k):
        return rcopy(msbuf.at[fwd(k)], msrecv.at[k], gsend.at[2 * group + k], grecv.at[2 * group + k], cell(fwd(k)))

    def ma_copy(k, j):
        return rcopy(msall.at[j], msall.at[j], gsend.at[3 * group + k], grecv.at[3 * group + k], cell(fwd(k)))

    def nst_copy(k):
        return rcopy(nstbuf, nstrecv.at[k], tsend.at[9, k], trecv.at[9, k], (p, d, plane(k)))

    loop(group, lambda k: ns_copy(k).start())
    loop(group, lambda k: ms_copy(k).start())
    loop(group, lambda k: ns_copy(k).wait_recv())
    ns = nsbuf[...]
    for k in range(1, group):
        ns = ns + nsrecv[k]
    nstbuf[...] = ns
    loop(nt, lambda k: nst_copy(k).start())
    loop(group, lambda k: ms_copy(k).wait_recv())
    ms = msbuf[slot].astype(F32)
    for k in range(1, group):
        ms = ms + msrecv[k].astype(F32)
    msall[pl.ds(slot, 1)] = ms.astype(BF)[None]
    loop(group, lambda k: ma_copy(k, slot).start())
    loop(nt, lambda k: nst_copy(k).wait_recv())
    for k in range(1, nt):
        ns = ns + nstrecv[k]
    rate = jnp.sqrt(width / (ns[0:1, 0:1] + 1e-06))
    loop(group, lambda k: ma_copy(k, back(k)).wait_recv())
    mall = msall[...].astype(F32).reshape(2 * tokens, -1)
    first = (2.0 * grad.astype(F32) - 0.5 * rate * mall[:tokens]).astype(BF)
    second = (-2.0 * hid.astype(F32) - 0.5 * rate * mall[tokens:]).astype(BF)
    s1 = dot(emb_t, first) + dot(vt, second)
    out_ref[...] = r_ref[...] - (0.5 * math.sqrt(width)) * rate * s1

    loop(nd, lambda k: r_copy(k, d).wait_send())
    x_copy.wait_send()
    loop(nd, lambda k: h_copy(k, d).wait_send())
    loop(nd, lambda k: e_copy(k, ring(k), d).wait_send())
    loop(nt, lambda k: vrs(k).wait_send())
    loop(nt, lambda k: vag(k, t).wait_send())
    loop(group, lambda k: ns_copy(k).wait_send())
    loop(group, lambda k: ms_copy(k).wait_send())
    loop(group, lambda k: ma_copy(k, slot).wait_send())
    loop(nt, lambda k: nst_copy(k).wait_send())


def solution(mesh):
    nd = mesh.shape["dp"]
    nt = mesh.shape["tensor"]

    def local(embedded, rotation, value_proj, output_proj, mid_exponent, cotangent):
        tg = embedded.shape[0]
        rows, cols = rotation.shape
        width = cols * nt
        units = value_proj.shape[2]
        half = units // 2
        own = tg // (nt // 2)
        group = 2 * nd
        vm = pltpu.VMEM
        dma = pltpu.SemaphoreType.DMA
        scratch = [
            vm((nd, rows, cols), BF),
            vm((tg, cols), BF),
            vm((tg, cols), BF),
            vm((nd, tg, cols), BF),
            vm((nd, tg, rows), BF),
            vm((nd, tg, cols), BF),
            vm((cols, units), BF),
            vm((8, units), F32),
            vm((8, units), F32),
            vm((2, tg, half), BF),
            vm((nt, own, half), BF),
            vm((2, tg, half + LANES), F32),
            vm((nt, own, half + LANES), F32),
            vm((nt, own, half + LANES), F32),
            vm((2, tg, half), BF),
            vm((2, tg, half + LANES), BF),
            vm((nt, own, half), BF),
            vm((2, tg, half + LANES), BF),
            vm((rows, nd * tg), BF),
            vm((nt, rows // nt, nd * tg), BF),
            vm((rows, nd * tg), BF),
            vm((group, tg, cols), BF),
            vm((group, tg, cols), BF),
            vm((group, tg, cols), BF),
            vm((8, LANES), F32),
            vm((group, 8, LANES), F32),
            vm((8, LANES), F32),
            vm((nt, 8, LANES), F32),
            dma((10, nt)),
            dma((10, nt)),
            dma((3, nd)),
            dma((3, nd)),
            dma((4 * group,)),
            dma((4 * group,)),
            dma((4,)),
            dma((4,)),
        ]
        return pl.pallas_call(
            functools.partial(kernel, nd, nt, float(width)),
            out_shape=jax.ShapeDtypeStruct((rows, cols), F32),
            in_specs=[pl.BlockSpec(memory_space=pltpu.VMEM)] * 6,
            out_specs=pl.BlockSpec(memory_space=pltpu.VMEM),
            scratch_shapes=scratch,
            compiler_params=pltpu.CompilerParams(
                collective_id=0, has_side_effects=True, vmem_limit_bytes=48 << 20
            ),
        )(embedded, rotation, value_proj, output_proj, mid_exponent, cotangent)

    return jax.shard_map(
        local,
        mesh=mesh,
        in_specs=(
            P("dp", "pipe"),
            P(("pipe", "dp"), "tensor"),
            P("pipe", "tensor", None),
            P("pipe", None, "tensor"),
            P("pipe", None),
            P("dp", "tensor"),
        ),
        out_specs=P(("pipe", "dp"), "tensor"),
        check_vma=False,
    )
```

```python
import functools
import math

import jax
import jax.numpy as jnp
from jax import lax
from jax.experimental import pallas as pl
from jax.experimental.pallas import tpu as pltpu
from jax.sharding import PartitionSpec as P

BF = jnp.bfloat16
F32 = jnp.float32
YT = jnp.float32
LANES = 128
NT_DIMS = (((1,), (1,)), ((), ()))


def dot(a, b):
    return jnp.dot(a, b, preferred_element_type=F32)


def dot_nt(a, b):
    return lax.dot_general(a, b, NT_DIMS, preferred_element_type=F32)


def up(a):
    return a.astype(F32)


def far_first(edge):
    cells = [(a, b) for a in range(edge) for b in range(edge) if a or b]
    return sorted(cells, key=lambda c: -min(c[0], edge - c[0]) - min(c[1], edge - c[1]))


def kernel(
    nd,
    nt,
    width,
    e_hbm,
    r_hbm,
    v_hbm,
    o_hbm,
    m_hbm,
    u_hbm,
    out_ref,
    e_ref,
    r_ref,
    v_ref,
    o_ref,
    m_ref,
    u_ref,
    rg,
    xpart,
    xrecv,
    xall,
    eall,
    gall,
    v1,
    bnd,
    bnd1,
    dcbuf,
    dc1recv,
    ybuf,
    y0recv,
    y1recv,
    cbuf,
    qbuf,
    dc0recv,
    q0buf,
    vpart,
    vrecv,
    vown,
    vall,
    gram,
    gramrecv,
    gramall,
    xgram,
    xgramrecv,
    xgramall,
    xx,
    yall,
    nsbuf,
    nsrecv,
    obuf,
    insem,
    tsend,
    trecv,
    rsend,
    rrecv,
    xsend,
    xrecv_sem,
    gsend,
    grecv,
    psend,
    precv,
):
    p = lax.axis_index("pipe")
    d = lax.axis_index("dp")
    t = lax.axis_index("tensor")
    tg = u_ref.shape[0]
    half = ybuf.shape[1] - LANES
    own = tg // (nt // 2)
    rows = rg.shape[1]
    group = 2 * nd
    slot = p * nd + d
    edge = math.isqrt(nt)
    tz, ty = t // edge, lax.rem(t, edge)
    tokens = nd * tg
    mine = tg // 2
    my_half = lax.rem(t, 2)

    def rcopy(src, dst, ssem, rsem, to):
        return pltpu.make_async_remote_copy(
            src_ref=src,
            dst_ref=dst,
            send_sem=ssem,
            recv_sem=rsem,
            device_id=to,
            device_id_type=pl.DeviceIdType.MESH,
        )

    others = []
    for a, b in far_first(edge):
        others.append(lax.rem(tz + a, edge) * edge + lax.rem(ty + b, edge))

    def to_plane(ph, src, dst):
        for i, j in enumerate(others):
            rcopy(src(j), dst(i), tsend.at[ph], trecv.at[ph], (p, d, j)).start()

    def plane_wait(ph, like):
        return rcopy(like, like, tsend.at[ph], trecv.at[ph], (p, d, others[-1]))

    def total(first, recv):
        acc = first.astype(F32)
        for i in range(nt - 1):
            acc = acc + recv[i].astype(F32)
        return acc

    def spot(j):
        return pl.ds(pl.multiple_of(lax.rem(j, 2) * tg + (j // 2) * own, own), own)

    def like(buf):
        return buf.at[pl.ds(0, (nt - 1) * own)]

    def rs_start(ph, buf, recv):
        to_plane(ph, lambda j: buf.at[spot(j)], lambda i: recv.at[i])

    def rs_total(ph, buf, recv):
        plane_wait(ph, recv).wait_recv()
        return total(buf[spot(t)], recv)

    def ag_start(ph, buf):
        to_plane(ph, lambda j: buf.at[spot(t)], lambda i: buf.at[spot(t)])

    def ag_wait(ph, buf):
        plane_wait(ph, like(buf)).wait_recv()

    def ring(k):
        return lax.rem(d + k, nd)

    partner = (1 - p, d, t)

    def to_ring(ph, src, dst):
        for k in (2, 1, 3):
            rcopy(src(ring(k)), dst(ring(k)), xsend.at[ph], xrecv_sem.at[ph], (p, ring(k), t)).start()

    def ring_wait(ph, like):
        return rcopy(like, like, xsend.at[ph], xrecv_sem.at[ph], (p, ring(1), t))

    loads = [
        pltpu.make_async_copy(src, dst, insem.at[i])
        for i, (src, dst) in enumerate(
            (
                (r_hbm, r_ref),
                (u_hbm, u_ref),
                (o_hbm, o_ref),
                (m_hbm, m_ref),
                (v_hbm, v_ref),
                (e_hbm, e_ref),
            )
        )
    ]
    for load in loads:
        load.start()

    bar = pltpu.get_barrier_semaphore()

    def greet(to):
        pl.semaphore_signal(bar, inc=1, device_id=to, device_id_type=pl.DeviceIdType.MESH)

    for j in others:
        greet((p, d, j))
    for k in range(1, nd):
        greet((p, ring(k), t))
        greet((1 - p, ring(k), t))
    greet(partner)

    loads[0].wait()
    rg[pl.ds(d, 1)] = (r_ref[...] * (1.0 / math.sqrt(width))).astype(BF)[None]
    pl.semaphore_wait(bar, nt - 1 + 2 * (nd - 1) + 1)

    hrow = rows // 2

    def r_half(s, h, to, i):
        blk = rg.at[s, pl.ds(h * hrow, hrow)]
        return rcopy(blk, blk, rsend.at[i], rrecv.at[i], (p, ring(to), t))

    ahead, behind = 1, nd - 1
    r_sends = [
        r_half(d, 0, ahead, 0),
        r_half(d, 1, behind, 1),
        r_half(d, 1, ahead, 2),
        r_half(d, 0, behind, 3),
    ]
    r_gets = [
        r_half(ring(behind), 0, ahead, 0),
        r_half(ring(ahead), 1, behind, 1),
        r_half(ring(behind), 1, ahead, 2),
        r_half(ring(ahead), 0, behind, 3),
    ]
    r_on = [r_half(ring(behind), 0, ahead, 4), r_half(ring(ahead), 1, behind, 5)]
    r_far = [r_half(ring(2), 0, ahead, 4), r_half(ring(2), 1, behind, 5)]
    for c in r_sends:
        c.start()
    for load in loads[1:]:
        load.wait()

    v1_copy = rcopy(v_ref.at[0], v1, psend.at[0], precv.at[0], partner)
    b1_copy = rcopy(bnd, bnd1, psend.at[1], precv.at[1], partner)
    d1_copy = rcopy(dcbuf, dcbuf, psend.at[2], precv.at[2], partner)
    x_copy = rcopy(xpart, xrecv, psend.at[3], precv.at[3], partner)
    xx_copy = rcopy(xgramall.at[0, pl.ds(0, mine)], xx, psend.at[4], precv.at[4], partner)
    g_copy = rcopy(gall.at[d], gall.at[d], psend.at[5], precv.at[5], partner)

    bnd[...] = jnp.broadcast_to(jnp.exp2(m_ref[...].astype(F32)), bnd.shape)

    def store_dc(part):
        dcbuf[:tg] = part[:, :half].astype(BF)
        dcbuf[tg:] = part[:, half:].astype(BF)

    @pl.when(p == 1)
    def _():
        store_dc(dot_nt(u_ref[...], o_ref[0]))
        d1_copy.start()
        b1_copy.start()
        v1_copy.start()

    @pl.when(p == 0)
    def _():
        d1_copy.wait_recv()
        rs_start(0, dcbuf, dc1recv)

    def e_dot(s):
        return dot(e_ref[:, pl.ds(pl.multiple_of(s * rows, LANES), rows)], rg[s])

    r_gets[0].wait_recv()
    r_on[0].start()
    r_gets[1].wait_recv()
    r_on[1].start()
    part = e_dot(d)
    r_gets[2].wait_recv()
    r_gets[3].wait_recv()
    part = part + e_dot(ring(1)) + e_dot(ring(3))
    r_far[0].wait_recv()
    r_far[1].wait_recv()
    part = part + e_dot(ring(2))
    xpart[...] = part.astype(BF)
    x_copy.start()
    x_copy.wait_recv()
    xall[pl.ds(d, 1)] = (up(xpart[...]) + up(xrecv[...])).astype(BF)[None]

    def share_inputs():
        to_ring(0, lambda j: xall.at[d], lambda j: xall.at[d])
        to_ring(
            1,
            lambda j: e_ref.at[:, pl.ds(pl.multiple_of(j * rows, LANES), rows)],
            lambda j: eall.at[d],
        )
        eall[pl.ds(d, 1)] = e_ref[:, pl.ds(pl.multiple_of(d * rows, LANES), rows)][None]

    gcol = tokens // edge

    def gspot(buf, j):
        grow = buf.shape[1] // edge
        return (
            slice(None),
            pl.ds(pl.multiple_of((j // edge) * grow, grow), grow),
            pl.ds(pl.multiple_of(lax.rem(j, edge) * gcol, gcol), gcol),
        )

    def gram_start(ph, buf, recv):
        to_plane(ph, lambda j: buf.at[gspot(buf, j)], lambda i: recv.at[i])

    def gram_turn(ph, buf, recv, full):
        plane_wait(ph, recv).wait_recv()
        full[gspot(full, t)] = total(buf[gspot(buf, t)], recv).astype(BF)
        blk = full.at[gspot(full, t)]
        to_plane(ph + 1, lambda j: blk, lambda i: blk)

    @pl.when(p == 0)
    def _():
        def two_parts(col):
            hi = up(col.astype(BF))
            shape = (col.shape[0], LANES)
            lane = lax.broadcasted_iota(jnp.int32, shape, 1)
            return jnp.where(lane < LANES // 2, jnp.broadcast_to(hi, shape), jnp.broadcast_to(col - hi, shape))

        def one_part(lanes):
            return jnp.sum(lanes, axis=1, keepdims=True) * (2.0 / LANES)

        def store_y(y, h):
            hf = up(h)
            sq = two_parts(jnp.sum(hf * hf, axis=1, keepdims=True)).astype(YT)
            ybuf[:tg, :half] = y[:, :half].astype(YT)
            ybuf[tg:, :half] = y[:, half:].astype(YT)
            ybuf[:tg, half:] = sq
            ybuf[tg:, half:] = sq

        def pick(b):
            return jnp.where(my_half == 0, b[0:1, :half], b[0:1, half:])

        def norm(tot):
            return lax.rsqrt(one_part(tot[:, half:]) / width + 1e-05)

        def gate(tot, dc, inv, bound, buf):
            y = tot[:, :half]
            z = inv * y
            inside = (z >= -8.0 * bound) & (z <= 7.0 * bound)
            q = (inv * jnp.where(inside, dc, 0.0)).astype(BF)
            coef = inv * inv / width * jnp.sum(up(q) * y, axis=1, keepdims=True)
            buf[spot(t), :half] = q
            buf[spot(t), half:] = two_parts(coef).astype(BF)

        def grad_in(buf, w):
            lin = dot_nt(buf[:tg, :half], w[:, :half]) + dot_nt(buf[tg:, :half], w[:, half:])
            return lin, one_part(up(buf[:tg, half:]) + up(buf[tg:, half:]))

        h0 = xall[d]
        store_y(dot(h0, v_ref[0]), h0)
        rs_start(1, ybuf, y0recv)
        share_inputs()
        tot0 = rs_total(1, ybuf, y0recv)
        inv0 = norm(tot0)
        bound0 = pick(bnd)
        cbuf[spot(t)] = jnp.clip(inv0 * tot0[:, :half], -8.0 * bound0, 7.0 * bound0).astype(BF)
        ag_start(2, cbuf)
        plane_wait(1, like(ybuf)).wait_send()
        ag_wait(2, cbuf)
        wo = o_ref[0]
        h1 = (up(xall[d]) + dot(cbuf[:tg], wo[:half]) + dot(cbuf[tg:], wo[half:])).astype(BF)
        v1_copy.wait_recv()
        b1_copy.wait_recv()
        store_y(dot(h1, v1[...]), h1)
        rs_start(3, ybuf, y1recv)
        dc1 = rs_total(0, dcbuf, dc1recv)
        plane_wait(0, like(dcbuf)).wait_send()
        tot1 = rs_total(3, ybuf, y1recv)
        gate(tot1, dc1, norm(tot1), pick(bnd1), qbuf)
        ag_start(4, qbuf)
        ag_wait(4, qbuf)
        lin, coef = grad_in(qbuf, v1[...])
        u1 = (up(u_ref[...]) + lin - coef * up(h1)).astype(BF)
        store_dc(dot_nt(u1, o_ref[0]))
        rs_start(5, dcbuf, dc0recv)
        dc0 = rs_total(5, dcbuf, dc0recv)
        gate(tot0, dc0, inv0, bound0, q0buf)
        ag_start(6, q0buf)
        ag_wait(6, q0buf)
        lin, coef = grad_in(q0buf, v_ref[0])
        gall[pl.ds(d, 1)] = (up(u1) + lin - coef * up(xall[d])).astype(BF)[None]
        g_copy.start()
        for i in range(2):
            for k in (2, 1, 3):
                rcopy(gall.at[d], gall.at[d], gsend.at[i], grecv.at[i], (i, ring(k), t)).start()

    @pl.when(p == 1)
    def _():
        share_inputs()
        ring_wait(0, xall.at[pl.ds(0, nd - 1)]).wait_recv()
        xgram[0] = dot_nt(xall[d], xall[...].reshape(tokens, xall.shape[2])).astype(BF)
        gram_start(10, xgram, xgramrecv)
        gram_turn(10, xgram, xgramrecv, xgramall)
        plane_wait(11, xgramrecv).wait_recv()
        xx[...] = xgramall[0, pl.ds(mine, mine)]
        xx_copy.start()
        g_copy.wait_recv()

    vsum = dot_nt(rg[...].reshape(nd * rows, rg.shape[2]), gall[d]).astype(BF)
    vpart[...] = vsum.reshape(nd, rows, tg)
    vrow = rows // nt

    def vspot(j):
        return pl.ds(pl.multiple_of(j * vrow, vrow), vrow)

    to_plane(7, lambda j: vpart.at[:, vspot(j)], lambda i: vrecv.at[i])

    my_rows = pl.ds(pl.multiple_of(p * mine, mine), mine)
    g_three = gall.at[pl.ds(0, nd - 1)]

    @pl.when(p == 0)
    def _():
        ring_wait(0, xall.at[pl.ds(0, nd - 1)]).wait_recv()
        rcopy(g_three, g_three, gsend.at[0], grecv.at[0], partner).wait_recv()

    @pl.when(p == 1)
    def _():
        rcopy(g_three, g_three, gsend.at[1], grecv.at[1], partner).wait_recv()

    hid = xall[...].reshape(tokens, xall.shape[2])
    g_mine = gall[d, my_rows]
    x_mine = xall[d, my_rows]
    grad = gall[...].reshape(tokens, gall.shape[2])
    gram[0] = dot_nt(g_mine, hid).astype(BF)
    gram[1] = dot_nt(g_mine, grad).astype(BF)
    gram[2] = dot_nt(x_mine, grad).astype(BF)
    gram_start(8, gram, gramrecv)

    plane_wait(7, vrecv).wait_recv()
    vown[...] = total(vpart[:, vspot(t)], vrecv).astype(BF)
    vmine = (vspot(t), pl.ds(pl.multiple_of(d * tg, tg), tg))
    to_ring(2, lambda j: vown.at[j], lambda j: vall.at[vmine])
    vall[vmine] = vown[d]

    gram_turn(8, gram, gramrecv, gramall)
    v_three = vown.at[pl.ds(0, nd - 1)]
    ring_wait(2, v_three).wait_recv()
    to_plane(12, lambda j: vall.at[vspot(t)], lambda i: vall.at[vspot(t)])

    e_three = eall.at[pl.ds(0, nd - 1)]
    ring_wait(1, e_three).wait_recv()
    emb_t = eall[...].reshape(tokens, rows).T
    front = 2.0 * dot(emb_t, grad)

    @pl.when(p == 0)
    def _():
        xx_copy.wait_recv()

    plane_wait(9, gramrecv).wait_recv()
    g_x, g_g, x_g, x_x = gramall[0], gramall[1], gramall[2], xx[...]

    def to_group(ph, src, dst):
        for k in (6, 2, 5, 7, 1, 3, 4):
            j = lax.rem(slot + k, group)
            rcopy(src, dst(k), gsend.at[ph], grecv.at[ph], (j // nd, lax.rem(j, nd), t)).start()

    def group_wait(ph, like):
        return rcopy(like, like, gsend.at[ph], grecv.at[ph], partner)

    nsbuf[...] = jnp.broadcast_to(8.0 * jnp.sum(up(x_x) * up(g_g) - up(g_x) * up(x_g)), nsbuf.shape)
    to_group(2, nsbuf, lambda k: nsrecv.at[k - 1])
    place = d * 2 + p
    yall[place, 0] = (2.0 * (dot(g_x, grad) - dot(g_g, hid))).astype(BF)
    yall[place, 1] = (2.0 * (dot(x_g, hid) - dot(x_x, grad))).astype(BF)
    to_group(3, yall.at[place], lambda k: yall.at[place])

    v_like = vall.at[pl.ds(0, (nt - 1) * vrow)]
    plane_wait(12, v_like).wait_recv()
    vt = vall[...]
    front = front - 2.0 * dot(vt, hid)
    group_wait(2, nsrecv).wait_recv()
    ns = nsbuf[...]
    for k in range(group - 1):
        ns = ns + nsrecv[k]
    rate = jnp.sqrt(width / (ns[0:1, 0:1] + 1e-06))
    scale = math.sqrt(width)
    obuf[...] = r_ref[...] - (0.5 * scale) * rate * front
    y_like = yall.at[pl.ds(0, group - 1)]
    group_wait(3, y_like).wait_recv()
    ya = yall[:, 0].reshape(tokens, -1)
    yb = yall[:, 1].reshape(tokens, -1)
    outs = []
    cut = rows // 4
    for i in range(4):
        blk = slice(i * cut, (i + 1) * cut)
        last = dot(emb_t[blk], ya) + dot(vt[blk], yb)
        obuf[blk] = obuf[blk] + (0.25 * scale) * (rate * rate) * last
        c = pltpu.make_async_copy(obuf.at[pl.ds(i * cut, cut)], out_ref.at[pl.ds(i * cut, cut)], insem.at[i])
        c.start()
        outs.append(c)

    for c in r_sends + r_on:
        c.wait_send()
    x_copy.wait_send()
    ring_wait(0, xall.at[pl.ds(0, nd - 1)]).wait_send()
    ring_wait(1, e_three).wait_send()
    ring_wait(2, v_three).wait_send()

    @pl.when(p == 0)
    def _():
        plane_wait(2, like(cbuf)).wait_send()
        plane_wait(3, like(ybuf)).wait_send()
        plane_wait(4, like(qbuf)).wait_send()
        plane_wait(5, like(dcbuf)).wait_send()
        plane_wait(6, like(q0buf)).wait_send()
        g_copy.wait_send()
        rcopy(g_three, g_three, gsend.at[0], grecv.at[0], partner).wait_send()
        rcopy(g_three, g_three, gsend.at[1], grecv.at[1], partner).wait_send()

    @pl.when(p == 1)
    def _():
        d1_copy.wait_send()
        b1_copy.wait_send()
        v1_copy.wait_send()
        plane_wait(10, xgramrecv).wait_send()
        plane_wait(11, xgramrecv).wait_send()
        xx_copy.wait_send()

    plane_wait(7, vrecv).wait_send()
    plane_wait(8, gramrecv).wait_send()
    plane_wait(9, gramrecv).wait_send()
    plane_wait(12, v_like).wait_send()
    group_wait(2, nsrecv).wait_send()
    group_wait(3, y_like).wait_send()
    for c in outs:
        c.wait()


def solution(mesh):
    nd = mesh.shape["dp"]
    nt = mesh.shape["tensor"]

    def local(embedded, rotation, value_proj, output_proj, mid_exponent, cotangent):
        tg = embedded.shape[0]
        rows, cols = rotation.shape
        width = cols * nt
        units = value_proj.shape[2]
        half = units // 2
        own = tg // (nt // 2)
        group = 2 * nd
        edge = math.isqrt(nt)
        mine = tg // 2
        tokens = nd * tg
        vm = pltpu.VMEM
        dma = pltpu.SemaphoreType.DMA
        scratch = [
            vm(embedded.shape, BF),
            vm(rotation.shape, F32),
            vm(value_proj.shape, BF),
            vm(output_proj.shape, BF),
            vm(mid_exponent.shape, jnp.int32),
            vm(cotangent.shape, BF),
            vm((nd, rows, cols), BF),
            vm((tg, cols), BF),
            vm((tg, cols), BF),
            vm((nd, tg, cols), BF),
            vm((nd, tg, rows), BF),
            vm((nd, tg, cols), BF),
            vm((cols, units), BF),
            vm((8, units), F32),
            vm((8, units), F32),
            vm((2 * tg, half), BF),
            vm((nt - 1, own, half), BF),
            vm((2 * tg, half + LANES), YT),
            vm((nt - 1, own, half + LANES), YT),
            vm((nt - 1, own, half + LANES), YT),
            vm((2 * tg, half), BF),
            vm((2 * tg, half + LANES), BF),
            vm((nt - 1, own, half), BF),
            vm((2 * tg, half + LANES), BF),
            vm((nd, rows, tg), BF),
            vm((nt - 1, nd, rows // nt, tg), BF),
            vm((nd, rows // nt, tg), BF),
            vm((rows, tokens), BF),
            vm((3, mine, tokens), BF),
            vm((nt - 1, 3, mine // edge, tokens // edge), BF),
            vm((3, mine, tokens), BF),
            vm((1, tg, tokens), BF),
            vm((nt - 1, 1, tg // edge, tokens // edge), BF),
            vm((1, tg, tokens), BF),
            vm((mine, tokens), BF),
            vm((group, 2, mine, cols), BF),
            vm((8, LANES), F32),
            vm((group - 1, 8, LANES), F32),
            vm((rows, cols), F32),
            dma((6,)),
            dma((13,)),
            dma((13,)),
            dma((6,)),
            dma((6,)),
            dma((3,)),
            dma((3,)),
            dma((4,)),
            dma((4,)),
            dma((6,)),
            dma((6,)),
        ]
        return pl.pallas_call(
            functools.partial(kernel, nd, nt, float(width)),
            out_shape=jax.ShapeDtypeStruct((rows, cols), F32),
            in_specs=[pl.BlockSpec(memory_space=pltpu.HBM)] * 6,
            out_specs=pl.BlockSpec(memory_space=pltpu.HBM),
            scratch_shapes=scratch,
            compiler_params=pltpu.CompilerParams(
                collective_id=0, has_side_effects=True, vmem_limit_bytes=67043328
            ),
        )(embedded, rotation, value_proj, output_proj, mid_exponent, cotangent)

    return jax.shard_map(
        local,
        mesh=mesh,
        in_specs=(
            P("dp", "pipe"),
            P(("pipe", "dp"), "tensor"),
            P("pipe", "tensor", None),
            P("pipe", None, "tensor"),
            P("pipe", None),
            P("dp", "tensor"),
        ),
        out_specs=P(("pipe", "dp"), "tensor"),
        check_vma=False,
    )
```

```python
import functools
import math

import jax
import jax.numpy as jnp
from jax import lax
from jax.experimental import pallas as pl
from jax.experimental.pallas import tpu as pltpu
from jax.sharding import PartitionSpec as P

BF = jnp.bfloat16
F32 = jnp.float32
YT = jnp.float32
LANES = 128
NT_DIMS = (((1,), (1,)), ((), ()))


def dot(a, b):
    return jnp.dot(a, b, preferred_element_type=F32)


def dot_nt(a, b):
    return lax.dot_general(a, b, NT_DIMS, preferred_element_type=F32)


def up(a):
    return a.astype(F32)


def far_first(edge):
    cells = [(a, b) for a in range(edge) for b in range(edge) if a or b]
    return sorted(cells, key=lambda c: -min(c[0], edge - c[0]) - min(c[1], edge - c[1]))


def kernel(
    nd,
    nt,
    width,
    e_hbm,
    r_hbm,
    v_hbm,
    o_hbm,
    m_hbm,
    u_hbm,
    out_ref,
    e_ref,
    r_ref,
    v_ref,
    o_ref,
    m_ref,
    u_ref,
    rg,
    xpart,
    xrecv,
    xall,
    eall,
    gall,
    v1,
    bnd,
    bnd1,
    dcbuf,
    dc1recv,
    e2buf,
    e2recv,
    hobuf,
    horecv,
    pbuf,
    pbrecv,
    pall,
    ybuf,
    y0recv,
    y1recv,
    cbuf,
    qbuf,
    q0buf,
    vpart,
    vrecv,
    vown,
    vall,
    gram,
    gramrecv,
    gramall,
    xgram,
    xgramrecv,
    xgramall,
    xx,
    yall,
    nsbuf,
    nsrecv,
    obuf,
    insem,
    tsend,
    trecv,
    rsend,
    rrecv,
    xsend,
    xrecv_sem,
    gsend,
    grecv,
    psend,
    precv,
):
    p = lax.axis_index("pipe")
    d = lax.axis_index("dp")
    t = lax.axis_index("tensor")
    tg = u_ref.shape[0]
    span = ybuf.shape[2]
    own = tg // 2
    rows = rg.shape[1]
    group = 2 * nd
    slot = p * nd + d
    edge = math.isqrt(nt)
    tz, ty = t // edge, lax.rem(t, edge)
    tokens = nd * tg
    mine = tg // 2
    my_side = lax.rem(t, 2)

    def rcopy(src, dst, ssem, rsem, to):
        return pltpu.make_async_remote_copy(
            src_ref=src,
            dst_ref=dst,
            send_sem=ssem,
            recv_sem=rsem,
            device_id=to,
            device_id_type=pl.DeviceIdType.MESH,
        )

    others = []
    for a, b in far_first(edge):
        others.append(lax.rem(tz + a, edge) * edge + lax.rem(ty + b, edge))

    def to_plane(ph, src, dst):
        for i, j in enumerate(others):
            rcopy(src(j), dst(i), tsend.at[ph], trecv.at[ph], (p, d, j)).start()

    def plane_wait(ph, like):
        return rcopy(like, like, tsend.at[ph], trecv.at[ph], (p, d, others[-1]))

    def total(first, recv):
        acc = first.astype(F32)
        for i in range(nt - 1):
            acc = acc + recv[i].astype(F32)
        return acc

    def split(buf, y):
        for j in range(nt):
            i, g = j % 2, j // 2
            buf[j, :own] = y[i * own : (i + 1) * own, g * span : (g + 1) * span].astype(buf.dtype)

    def side_of(buf, i):
        return jnp.concatenate([buf[2 * g + i, :own] for g in range(nt // 2)], axis=1)

    def join(buf):
        return jnp.concatenate([side_of(buf, 0), side_of(buf, 1)], axis=0)

    def like(buf):
        return buf.at[pl.ds(0, nt - 1)]

    def rs_start(ph, buf, recv):
        to_plane(ph, lambda j: buf.at[j], lambda i: recv.at[i])

    def rs_total(ph, buf, recv):
        plane_wait(ph, recv).wait_recv()
        return total(buf[t], recv)

    def ag_start(ph, buf):
        to_plane(ph, lambda j: buf.at[t], lambda i: buf.at[t])

    def ag_wait(ph, buf):
        plane_wait(ph, like(buf)).wait_recv()

    def ring(k):
        return lax.rem(d + k, nd)

    partner = (1 - p, d, t)

    def to_ring(ph, src, dst):
        for k in (2, 1, 3):
            rcopy(src(ring(k)), dst(ring(k)), xsend.at[ph], xrecv_sem.at[ph], (p, ring(k), t)).start()

    def ring_wait(ph, like):
        return rcopy(like, like, xsend.at[ph], xrecv_sem.at[ph], (p, ring(1), t))

    loads = [
        pltpu.make_async_copy(src, dst, insem.at[i])
        for i, (src, dst) in enumerate(
            (
                (r_hbm, r_ref),
                (u_hbm, u_ref),
                (o_hbm, o_ref),
                (m_hbm, m_ref),
                (v_hbm, v_ref),
                (e_hbm, e_ref),
            )
        )
    ]
    for load in loads:
        load.start()

    bar = pltpu.get_barrier_semaphore()

    def greet(to):
        pl.semaphore_signal(bar, inc=1, device_id=to, device_id_type=pl.DeviceIdType.MESH)

    for j in others:
        greet((p, d, j))
    for k in range(1, nd):
        greet((p, ring(k), t))
        greet((1 - p, ring(k), t))
    greet(partner)

    loads[0].wait()
    rg[pl.ds(d, 1)] = (r_ref[...] * (1.0 / math.sqrt(width))).astype(BF)[None]
    pl.semaphore_wait(bar, nt - 1 + 2 * (nd - 1) + 1)

    hrow = rows // 2

    def r_half(s, h, to, i):
        blk = rg.at[s, pl.ds(h * hrow, hrow)]
        return rcopy(blk, blk, rsend.at[i], rrecv.at[i], (p, ring(to), t))

    ahead, behind = 1, nd - 1
    r_sends = [
        r_half(d, 0, ahead, 0),
        r_half(d, 1, behind, 1),
        r_half(d, 1, ahead, 2),
        r_half(d, 0, behind, 3),
    ]
    r_gets = [
        r_half(ring(behind), 0, ahead, 0),
        r_half(ring(ahead), 1, behind, 1),
        r_half(ring(behind), 1, ahead, 2),
        r_half(ring(ahead), 0, behind, 3),
    ]
    r_on = [r_half(ring(behind), 0, ahead, 4), r_half(ring(ahead), 1, behind, 5)]
    r_far = [r_half(ring(2), 0, ahead, 4), r_half(ring(2), 1, behind, 5)]
    for c in r_sends:
        c.start()
    for load in loads[1:]:
        load.wait()

    v1_copy = rcopy(v_ref.at[0], v1, psend.at[0], precv.at[0], partner)
    b1_copy = rcopy(bnd, bnd1, psend.at[1], precv.at[1], partner)
    d1_copy = rcopy(dcbuf, dcbuf, psend.at[2], precv.at[2], partner)
    x_copy = rcopy(xpart, xrecv, psend.at[3], precv.at[3], partner)
    xx_copy = rcopy(xgramall.at[0, pl.ds(0, mine)], xx, psend.at[4], precv.at[4], partner)
    g_copy = rcopy(gall.at[d], gall.at[d], psend.at[5], precv.at[5], partner)

    bnd[...] = jnp.broadcast_to(jnp.exp2(m_ref[...].astype(F32)), bnd.shape)

    @pl.when(p == 1)
    def _():
        v1_copy.start()
        split(dcbuf, dot_nt(u_ref[...], o_ref[0]))
        d1_copy.start()
        b1_copy.start()

    @pl.when(p == 0)
    def _():
        split(e2buf, dot_nt(u_ref[...], o_ref[0]))
        v1_copy.wait_recv()
        quarter = pbuf.shape[2]
        cross = dot(o_ref[0], v1[:, pl.ds(pl.multiple_of(d * quarter, quarter), quarter)])
        pbuf[...] = cross.astype(BF).reshape(pbuf.shape)
        to_plane(13, lambda j: pbuf.at[j // 2], lambda i: pbrecv.at[i])
        rs_start(5, e2buf, e2recv)
        d1_copy.wait_recv()
        rs_start(0, dcbuf, dc1recv)

    def e_dot(s):
        return dot(e_ref[:, pl.ds(pl.multiple_of(s * rows, LANES), rows)], rg[s])

    r_gets[0].wait_recv()
    r_on[0].start()
    r_gets[1].wait_recv()
    r_on[1].start()
    part = e_dot(d)
    r_gets[2].wait_recv()
    r_gets[3].wait_recv()
    part = part + e_dot(ring(1)) + e_dot(ring(3))
    r_far[0].wait_recv()
    r_far[1].wait_recv()
    part = part + e_dot(ring(2))
    xpart[...] = part.astype(BF)
    x_copy.start()
    x_copy.wait_recv()
    xall[pl.ds(d, 1)] = (up(xpart[...]) + up(xrecv[...])).astype(BF)[None]

    def share_inputs():
        to_ring(0, lambda j: xall.at[d], lambda j: xall.at[d])
        to_ring(
            1,
            lambda j: e_ref.at[:, pl.ds(pl.multiple_of(j * rows, LANES), rows)],
            lambda j: eall.at[d],
        )
        eall[pl.ds(d, 1)] = e_ref[:, pl.ds(pl.multiple_of(d * rows, LANES), rows)][None]

    gcol = tokens // edge

    def gspot(buf, j):
        grow = buf.shape[1] // edge
        return (
            slice(None),
            pl.ds(pl.multiple_of((j // edge) * grow, grow), grow),
            pl.ds(pl.multiple_of(lax.rem(j, edge) * gcol, gcol), gcol),
        )

    def gram_start(ph, buf, recv):
        to_plane(ph, lambda j: buf.at[gspot(buf, j)], lambda i: recv.at[i])

    def gram_turn(ph, buf, recv, full):
        plane_wait(ph, recv).wait_recv()
        full[gspot(full, t)] = total(buf[gspot(buf, t)], recv).astype(BF)
        blk = full.at[gspot(full, t)]
        to_plane(ph + 1, lambda j: blk, lambda i: blk)

    @pl.when(p == 0)
    def _():
        def diagonal():
            shape = (own, LANES)
            return lax.broadcasted_iota(jnp.int32, shape, 0) == lax.broadcasted_iota(jnp.int32, shape, 1)

        def to_row(col):
            return jnp.sum(jnp.where(diagonal(), col, 0.0), axis=0, keepdims=True)

        def to_col(row):
            return jnp.sum(jnp.where(diagonal(), row, 0.0), axis=1, keepdims=True)

        def store_y(y, h):
            split(ybuf, y)
            hf = up(h)
            sq = jnp.sum(hf * hf, axis=1, keepdims=True)
            for i in range(2):
                tile = jnp.broadcast_to(to_row(sq[i * own : (i + 1) * own]), (8, LANES))
                for g in range(nt // 2):
                    ybuf[2 * g + i, own:] = tile

        def pick(b):
            g = t // 2
            out = b[0:1, :span]
            for i in range(1, nt // 2):
                out = jnp.where(g == i, b[0:1, i * span : (i + 1) * span], out)
            return out

        def norm(tot):
            return lax.rsqrt(to_col(tot[own : own + 1]) / width + 1e-05)

        def gate(tot, dc, inv, bound, buf):
            y = tot[:own]
            z = inv * y
            inside = (z >= -8.0 * bound) & (z <= 7.0 * bound)
            q = (inv * jnp.where(inside, dc, 0.0)).astype(BF)
            coef = to_row(inv * inv / width * jnp.sum(up(q) * y, axis=1, keepdims=True))
            hi = up(coef.astype(BF))
            row = lax.broadcasted_iota(jnp.int32, (16, LANES), 0)
            buf[t, :own] = q
            buf[t, own:] = jnp.where(row == 0, hi, jnp.where(row == 1, coef - hi, 0.0)).astype(BF)

        def coef_of(buf, i):
            ext = up(buf[i, own:])
            for g in range(1, nt // 2):
                ext = ext + up(buf[2 * g + i, own:])
            return to_col(jnp.sum(ext, axis=0, keepdims=True))

        def grad_in(buf, w):
            coef = jnp.concatenate([coef_of(buf, 0), coef_of(buf, 1)], axis=0)
            return dot_nt(join(buf), w), coef

        h0 = xall[d]
        store_y(dot(h0, v_ref[0]), h0)
        rs_start(1, ybuf, y0recv)
        share_inputs()
        plane_wait(13, pbrecv).wait_recv()
        pall[pl.ds(d, 1)] = total(pbuf[t // 2], pbrecv).astype(BF)[None]
        to_ring(3, lambda j: pall.at[d], lambda j: pall.at[d])
        tot0 = rs_total(1, ybuf, y0recv)
        inv0 = norm(tot0)
        bound0 = pick(bnd)
        cbuf[t] = jnp.clip(inv0 * tot0[:own], -8.0 * bound0, 7.0 * bound0).astype(BF)
        ag_start(2, cbuf)
        plane_wait(1, like(ybuf)).wait_send()
        dc1 = rs_total(0, dcbuf, dc1recv)
        e2 = rs_total(5, e2buf, e2recv)
        b1_copy.wait_recv()
        bound1 = pick(bnd1)
        ag_wait(2, cbuf)
        h1 = (up(xall[d]) + dot(join(cbuf), o_ref[0])).astype(BF)
        store_y(dot(h1, v1[...]), h1)
        rs_start(3, ybuf, y1recv)
        split(hobuf, dot_nt(h1, o_ref[0]))
        rs_start(14, hobuf, horecv)
        tot1 = rs_total(3, ybuf, y1recv)
        gate(tot1, dc1, norm(tot1), bound1, qbuf)
        ag_start(4, qbuf)
        ho = rs_total(14, hobuf, horecv)
        p_three = pall.at[pl.ds(0, nd - 1)]
        ring_wait(3, p_three).wait_recv()
        ag_wait(4, qbuf)
        q1 = side_of(qbuf, my_side)
        quarter = pall.shape[2]
        dc0 = e2 - coef_of(qbuf, my_side) * ho
        for i in range(nd):
            dc0 = dc0 + dot_nt(q1[:, i * quarter : (i + 1) * quarter], pall[i])
        gate(tot0, dc0, inv0, bound0, q0buf)
        ag_start(6, q0buf)
        lin, coef = grad_in(qbuf, v1[...])
        u1 = (up(u_ref[...]) + lin - coef * up(h1)).astype(BF)
        ag_wait(6, q0buf)
        lin, coef = grad_in(q0buf, v_ref[0])
        gall[pl.ds(d, 1)] = (up(u1) + lin - coef * up(xall[d])).astype(BF)[None]
        g_copy.start()
        for i in range(2):
            for k in (2, 1, 3):
                rcopy(gall.at[d], gall.at[d], gsend.at[i], grecv.at[i], (i, ring(k), t)).start()

    @pl.when(p == 1)
    def _():
        share_inputs()
        ring_wait(0, xall.at[pl.ds(0, nd - 1)]).wait_recv()
        xgram[0] = dot_nt(xall[d], xall[...].reshape(tokens, xall.shape[2])).astype(BF)
        gram_start(10, xgram, xgramrecv)
        gram_turn(10, xgram, xgramrecv, xgramall)
        plane_wait(11, xgramrecv).wait_recv()
        xx[...] = xgramall[0, pl.ds(mine, mine)]
        xx_copy.start()
        g_copy.wait_recv()

    vsum = dot_nt(rg[...].reshape(nd * rows, rg.shape[2]), gall[d]).astype(BF)
    vpart[...] = vsum.reshape(nd, rows, tg)
    vrow = rows // nt

    def vspot(j):
        return pl.ds(pl.multiple_of(j * vrow, vrow), vrow)

    to_plane(7, lambda j: vpart.at[:, vspot(j)], lambda i: vrecv.at[i])

    my_rows = pl.ds(pl.multiple_of(p * mine, mine), mine)
    g_three = gall.at[pl.ds(0, nd - 1)]

    @pl.when(p == 0)
    def _():
        ring_wait(0, xall.at[pl.ds(0, nd - 1)]).wait_recv()
        rcopy(g_three, g_three, gsend.at[0], grecv.at[0], partner).wait_recv()

    @pl.when(p == 1)
    def _():
        rcopy(g_three, g_three, gsend.at[1], grecv.at[1], partner).wait_recv()

    hid = xall[...].reshape(tokens, xall.shape[2])
    g_mine = gall[d, my_rows]
    x_mine = xall[d, my_rows]
    grad = gall[...].reshape(tokens, gall.shape[2])
    gram[0] = dot_nt(g_mine, hid).astype(BF)
    gram[1] = dot_nt(g_mine, grad).astype(BF)
    gram[2] = dot_nt(x_mine, grad).astype(BF)
    gram_start(8, gram, gramrecv)

    plane_wait(7, vrecv).wait_recv()
    vown[...] = total(vpart[:, vspot(t)], vrecv).astype(BF)
    vmine = (vspot(t), pl.ds(pl.multiple_of(d * tg, tg), tg))
    to_ring(2, lambda j: vown.at[j], lambda j: vall.at[vmine])
    vall[vmine] = vown[d]

    gram_turn(8, gram, gramrecv, gramall)
    v_three = vown.at[pl.ds(0, nd - 1)]
    ring_wait(2, v_three).wait_recv()
    to_plane(12, lambda j: vall.at[vspot(t)], lambda i: vall.at[vspot(t)])

    e_three = eall.at[pl.ds(0, nd - 1)]
    ring_wait(1, e_three).wait_recv()
    emb_t = eall[...].reshape(tokens, rows).T
    front = 2.0 * dot(emb_t, grad)

    @pl.when(p == 0)
    def _():
        xx_copy.wait_recv()

    plane_wait(9, gramrecv).wait_recv()
    g_x, g_g, x_g, x_x = gramall[0], gramall[1], gramall[2], xx[...]

    def to_group(ph, src, dst):
        for k in (6, 2, 5, 7, 1, 3, 4):
            j = lax.rem(slot + k, group)
            rcopy(src, dst(k), gsend.at[ph], grecv.at[ph], (j // nd, lax.rem(j, nd), t)).start()

    def group_wait(ph, like):
        return rcopy(like, like, gsend.at[ph], grecv.at[ph], partner)

    nsbuf[...] = jnp.broadcast_to(8.0 * jnp.sum(up(x_x) * up(g_g) - up(g_x) * up(x_g)), nsbuf.shape)
    to_group(2, nsbuf, lambda k: nsrecv.at[k - 1])
    place = d * 2 + p
    yall[place, 0] = (2.0 * (dot(g_x, grad) - dot(g_g, hid))).astype(BF)
    yall[place, 1] = (2.0 * (dot(x_g, hid) - dot(x_x, grad))).astype(BF)
    to_group(3, yall.at[place], lambda k: yall.at[place])

    v_like = vall.at[pl.ds(0, (nt - 1) * vrow)]
    plane_wait(12, v_like).wait_recv()
    vt = vall[...]
    front = front - 2.0 * dot(vt, hid)
    group_wait(2, nsrecv).wait_recv()
    ns = nsbuf[...]
    for k in range(group - 1):
        ns = ns + nsrecv[k]
    rate = jnp.sqrt(width / (ns[0:1, 0:1] + 1e-06))
    scale = math.sqrt(width)
    obuf[...] = r_ref[...] - (0.5 * scale) * rate * front
    y_like = yall.at[pl.ds(0, group - 1)]
    group_wait(3, y_like).wait_recv()
    ya = yall[:, 0].reshape(tokens, -1)
    yb = yall[:, 1].reshape(tokens, -1)
    outs = []
    cut = rows // 4
    for i in range(4):
        blk = slice(i * cut, (i + 1) * cut)
        last = dot(emb_t[blk], ya) + dot(vt[blk], yb)
        obuf[blk] = obuf[blk] + (0.25 * scale) * (rate * rate) * last
        c = pltpu.make_async_copy(obuf.at[pl.ds(i * cut, cut)], out_ref.at[pl.ds(i * cut, cut)], insem.at[i])
        c.start()
        outs.append(c)

    for c in r_sends + r_on:
        c.wait_send()
    x_copy.wait_send()
    ring_wait(0, xall.at[pl.ds(0, nd - 1)]).wait_send()
    ring_wait(1, e_three).wait_send()
    ring_wait(2, v_three).wait_send()

    @pl.when(p == 0)
    def _():
        plane_wait(0, like(dcbuf)).wait_send()
        plane_wait(2, like(cbuf)).wait_send()
        plane_wait(3, like(ybuf)).wait_send()
        plane_wait(4, like(qbuf)).wait_send()
        plane_wait(5, like(e2buf)).wait_send()
        plane_wait(6, like(q0buf)).wait_send()
        plane_wait(13, pbrecv).wait_send()
        plane_wait(14, like(hobuf)).wait_send()
        ring_wait(3, pall.at[pl.ds(0, nd - 1)]).wait_send()
        g_copy.wait_send()
        rcopy(g_three, g_three, gsend.at[0], grecv.at[0], partner).wait_send()
        rcopy(g_three, g_three, gsend.at[1], grecv.at[1], partner).wait_send()

    @pl.when(p == 1)
    def _():
        d1_copy.wait_send()
        b1_copy.wait_send()
        v1_copy.wait_send()
        plane_wait(10, xgramrecv).wait_send()
        plane_wait(11, xgramrecv).wait_send()
        xx_copy.wait_send()

    plane_wait(7, vrecv).wait_send()
    plane_wait(8, gramrecv).wait_send()
    plane_wait(9, gramrecv).wait_send()
    plane_wait(12, v_like).wait_send()
    group_wait(2, nsrecv).wait_send()
    group_wait(3, y_like).wait_send()
    for c in outs:
        c.wait()


def solution(mesh):
    nd = mesh.shape["dp"]
    nt = mesh.shape["tensor"]

    def local(embedded, rotation, value_proj, output_proj, mid_exponent, cotangent):
        tg = embedded.shape[0]
        rows, cols = rotation.shape
        width = cols * nt
        units = value_proj.shape[2]
        own = tg // 2
        span = units // (nt // 2)
        group = 2 * nd
        edge = math.isqrt(nt)
        mine = tg // 2
        tokens = nd * tg
        vm = pltpu.VMEM
        dma = pltpu.SemaphoreType.DMA
        scratch = [
            vm(embedded.shape, BF),
            vm(rotation.shape, F32),
            vm(value_proj.shape, BF),
            vm(output_proj.shape, BF),
            vm(mid_exponent.shape, jnp.int32),
            vm(cotangent.shape, BF),
            vm((nd, rows, cols), BF),
            vm((tg, cols), BF),
            vm((tg, cols), BF),
            vm((nd, tg, cols), BF),
            vm((nd, tg, rows), BF),
            vm((nd, tg, cols), BF),
            vm((cols, units), BF),
            vm((8, units), F32),
            vm((8, units), F32),
            vm((nt, own, span), BF),
            vm((nt - 1, own, span), BF),
            vm((nt, own, span), BF),
            vm((nt - 1, own, span), BF),
            vm((nt, own, span), BF),
            vm((nt - 1, own, span), BF),
            vm((nt // 2, span, units // nd), BF),
            vm((nt - 1, span, units // nd), BF),
            vm((nd, span, units // nd), BF),
            vm((nt, own + 8, span), YT),
            vm((nt - 1, own + 8, span), YT),
            vm((nt - 1, own + 8, span), YT),
            vm((nt, own, span), BF),
            vm((nt, own + 16, span), BF),
            vm((nt, own + 16, span), BF),
            vm((nd, rows, tg), BF),
            vm((nt - 1, nd, rows // nt, tg), BF),
            vm((nd, rows // nt, tg), BF),
            vm((rows, tokens), BF),
            vm((3, mine, tokens), BF),
            vm((nt - 1, 3, mine // edge, tokens // edge), BF),
            vm((3, mine, tokens), BF),
            vm((1, tg, tokens), BF),
            vm((nt - 1, 1, tg // edge, tokens // edge), BF),
            vm((1, tg, tokens), BF),
            vm((mine, tokens), BF),
            vm((group, 2, mine, cols), BF),
            vm((8, LANES), F32),
            vm((group - 1, 8, LANES), F32),
            vm((rows, cols), F32),
            dma((6,)),
            dma((15,)),
            dma((15,)),
            dma((12,)),
            dma((12,)),
            dma((4,)),
            dma((4,)),
            dma((4,)),
            dma((4,)),
            dma((6,)),
            dma((6,)),
        ]
        return pl.pallas_call(
            functools.partial(kernel, nd, nt, float(width)),
            out_shape=jax.ShapeDtypeStruct((rows, cols), F32),
            in_specs=[pl.BlockSpec(memory_space=pltpu.HBM)] * 6,
            out_specs=pl.BlockSpec(memory_space=pltpu.HBM),
            scratch_shapes=scratch,
            compiler_params=pltpu.CompilerParams(
                collective_id=0, has_side_effects=True, vmem_limit_bytes=67043328
            ),
        )(embedded, rotation, value_proj, output_proj, mid_exponent, cotangent)

    return jax.shard_map(
        local,
        mesh=mesh,
        in_specs=(
            P("dp", "pipe"),
            P(("pipe", "dp"), "tensor"),
            P("pipe", "tensor", None),
            P("pipe", None, "tensor"),
            P("pipe", None),
            P("dp", "tensor"),
        ),
        out_specs=P(("pipe", "dp"), "tensor"),
        check_vma=False,
    )
```

```python
import functools
import math

import jax
import jax.numpy as jnp
from jax import lax
from jax.experimental import pallas as pl
from jax.experimental.pallas import tpu as pltpu
from jax.sharding import PartitionSpec as P

BF = jnp.bfloat16
F32 = jnp.float32
YT = jnp.float32
OT = jnp.float32
LANES = 128
NT_DIMS = (((1,), (1,)), ((), ()))


def dot(a, b):
    return jnp.dot(a, b, preferred_element_type=F32)


def dot_nt(a, b):
    return lax.dot_general(a, b, NT_DIMS, preferred_element_type=F32)


def up(a):
    return a.astype(F32)


def far_first(edge):
    cells = [(a, b) for a in range(edge) for b in range(edge) if a or b]
    return sorted(cells, key=lambda c: -min(c[0], edge - c[0]) - min(c[1], edge - c[1]))


def kernel(
    nd,
    nt,
    width,
    e_hbm,
    r_hbm,
    v_hbm,
    o_hbm,
    m_hbm,
    u_hbm,
    out_ref,
    e_ref,
    r_ref,
    v_ref,
    o_ref,
    m_ref,
    u_ref,
    rg,
    xpart,
    xrecv,
    xall,
    eall,
    gall,
    v1,
    bnd,
    bnd1,
    dcbuf,
    dc1recv,
    e2buf,
    e2recv,
    hobuf,
    horecv,
    pbuf,
    pbrecv,
    pall,
    ybuf,
    y0recv,
    y1recv,
    cbuf,
    qbuf,
    q0buf,
    vpart,
    vrecv,
    vown,
    vall,
    gram,
    gramrecv,
    gramall,
    xgram,
    xgramrecv,
    xgramall,
    xx,
    yall,
    nsbuf,
    nsrecv,
    insem,
    tsend,
    trecv,
    rsend,
    rrecv,
    xsend,
    xrecv_sem,
    gsend,
    grecv,
    psend,
    precv,
    ysend,
    yrecv,
    vasend,
    varecv,
):
    p = lax.axis_index("pipe")
    d = lax.axis_index("dp")
    t = lax.axis_index("tensor")
    tg = u_ref.shape[0]
    span = ybuf.shape[2]
    own = tg // 2
    rows = rg.shape[1]
    group = 2 * nd
    slot = p * nd + d
    edge = math.isqrt(nt)
    tz, ty = t // edge, lax.rem(t, edge)
    tokens = nd * tg
    mine = tg // 2
    my_side = lax.rem(t, 2)

    def rcopy(src, dst, ssem, rsem, to):
        return pltpu.make_async_remote_copy(
            src_ref=src,
            dst_ref=dst,
            send_sem=ssem,
            recv_sem=rsem,
            device_id=to,
            device_id_type=pl.DeviceIdType.MESH,
        )

    others = []
    for a, b in far_first(edge):
        others.append(lax.rem(tz + a, edge) * edge + lax.rem(ty + b, edge))

    def to_plane(ph, src, dst):
        for i, j in enumerate(others):
            rcopy(src(j), dst(i), tsend.at[ph], trecv.at[ph], (p, d, j)).start()

    def plane_wait(ph, like):
        return rcopy(like, like, tsend.at[ph], trecv.at[ph], (p, d, others[-1]))

    def total(first, recv):
        acc = first.astype(F32)
        for i in range(nt - 1):
            acc = acc + recv[i].astype(F32)
        return acc

    def split(buf, y):
        for j in range(nt):
            i, g = j % 2, j // 2
            buf[j, :own] = y[i * own : (i + 1) * own, g * span : (g + 1) * span].astype(buf.dtype)

    def side_of(buf, i):
        return jnp.concatenate([buf[2 * g + i, :own] for g in range(nt // 2)], axis=1)

    def join(buf):
        return jnp.concatenate([side_of(buf, 0), side_of(buf, 1)], axis=0)

    def like(buf):
        return buf.at[pl.ds(0, nt - 1)]

    def rs_start(ph, buf, recv):
        to_plane(ph, lambda j: buf.at[j], lambda i: recv.at[i])

    def rs_total(ph, buf, recv):
        plane_wait(ph, recv).wait_recv()
        return total(buf[t], recv)

    def ag_start(ph, buf):
        to_plane(ph, lambda j: buf.at[t], lambda i: buf.at[t])

    def ag_wait(ph, buf):
        plane_wait(ph, like(buf)).wait_recv()

    def ring(k):
        return lax.rem(d + k, nd)

    partner = (1 - p, d, t)

    def to_ring(ph, src, dst):
        for k in (2, 1, 3):
            rcopy(src(ring(k)), dst(ring(k)), xsend.at[ph], xrecv_sem.at[ph], (p, ring(k), t)).start()

    def ring_wait(ph, like):
        return rcopy(like, like, xsend.at[ph], xrecv_sem.at[ph], (p, ring(1), t))

    loads = [
        pltpu.make_async_copy(src, dst, insem.at[i])
        for i, (src, dst) in enumerate(
            (
                (r_hbm, r_ref),
                (u_hbm, u_ref),
                (o_hbm, o_ref),
                (m_hbm, m_ref),
                (v_hbm, v_ref),
                (e_hbm, e_ref),
            )
        )
    ]
    for load in loads:
        load.start()

    bar = pltpu.get_barrier_semaphore()

    def greet(to):
        pl.semaphore_signal(bar, inc=1, device_id=to, device_id_type=pl.DeviceIdType.MESH)

    for j in others:
        greet((p, d, j))
    for k in range(1, nd):
        greet((p, ring(k), t))
        greet((1 - p, ring(k), t))
    greet(partner)

    loads[0].wait()
    rg[pl.ds(d, 1)] = (r_ref[...] * (1.0 / math.sqrt(width))).astype(BF)[None]
    pl.semaphore_wait(bar, nt - 1 + 2 * (nd - 1) + 1)

    hrow = rows // 2

    def r_half(s, h, to, i):
        blk = rg.at[s, pl.ds(h * hrow, hrow)]
        return rcopy(blk, blk, rsend.at[i], rrecv.at[i], (p, ring(to), t))

    ahead, behind = 1, nd - 1
    r_sends = [
        r_half(d, 0, ahead, 0),
        r_half(d, 1, behind, 1),
        r_half(d, 1, ahead, 2),
        r_half(d, 0, behind, 3),
    ]
    r_gets = [
        r_half(ring(behind), 0, ahead, 0),
        r_half(ring(ahead), 1, behind, 1),
        r_half(ring(behind), 1, ahead, 2),
        r_half(ring(ahead), 0, behind, 3),
    ]
    r_on = [r_half(ring(behind), 0, ahead, 4), r_half(ring(ahead), 1, behind, 5)]
    r_far = [r_half(ring(2), 0, ahead, 4), r_half(ring(2), 1, behind, 5)]
    for c in r_sends:
        c.start()
    for load in loads[1:]:
        load.wait()

    v1_copy = rcopy(v_ref.at[0], v1, psend.at[0], precv.at[0], partner)
    b1_copy = rcopy(bnd, bnd1, psend.at[1], precv.at[1], partner)
    d1_copy = rcopy(dcbuf, dcbuf, psend.at[2], precv.at[2], partner)
    x_copy = rcopy(xpart, xrecv, psend.at[3], precv.at[3], partner)
    xx_copy = rcopy(xgramall.at[0, pl.ds(0, mine)], xx, psend.at[4], precv.at[4], partner)
    g_copy = rcopy(gall.at[d], gall.at[d], psend.at[5], precv.at[5], partner)

    bnd[...] = jnp.broadcast_to(jnp.exp2(m_ref[...].astype(F32)), bnd.shape)

    @pl.when(p == 1)
    def _():
        v1_copy.start()
        split(dcbuf, dot_nt(u_ref[...], o_ref[0]))
        d1_copy.start()
        b1_copy.start()

    @pl.when(p == 0)
    def _():
        split(e2buf, dot_nt(u_ref[...], o_ref[0]))
        v1_copy.wait_recv()
        quarter = pbuf.shape[2]
        cross = dot(o_ref[0], v1[:, pl.ds(pl.multiple_of(d * quarter, quarter), quarter)])
        pbuf[...] = cross.astype(BF).reshape(pbuf.shape)
        to_plane(13, lambda j: pbuf.at[j // 2], lambda i: pbrecv.at[i])
        rs_start(5, e2buf, e2recv)
        d1_copy.wait_recv()
        rs_start(0, dcbuf, dc1recv)

    def e_dot(s):
        return dot(e_ref[:, pl.ds(pl.multiple_of(s * rows, LANES), rows)], rg[s])

    r_gets[0].wait_recv()
    r_on[0].start()
    r_gets[1].wait_recv()
    r_on[1].start()
    part = e_dot(d)
    r_gets[2].wait_recv()
    r_gets[3].wait_recv()
    part = part + e_dot(ring(1)) + e_dot(ring(3))
    r_far[0].wait_recv()
    r_far[1].wait_recv()
    part = part + e_dot(ring(2))
    xpart[...] = part.astype(BF)
    x_copy.start()
    x_copy.wait_recv()
    xall[pl.ds(d, 1)] = (up(xpart[...]) + up(xrecv[...])).astype(BF)[None]

    def share_inputs():
        to_ring(0, lambda j: xall.at[d], lambda j: xall.at[d])
        to_ring(
            1,
            lambda j: e_ref.at[:, pl.ds(pl.multiple_of(j * rows, LANES), rows)],
            lambda j: eall.at[d],
        )
        eall[pl.ds(d, 1)] = e_ref[:, pl.ds(pl.multiple_of(d * rows, LANES), rows)][None]

    gcol = tokens // edge

    def gspot(buf, j):
        grow = buf.shape[1] // edge
        return (
            slice(None),
            pl.ds(pl.multiple_of((j // edge) * grow, grow), grow),
            pl.ds(pl.multiple_of(lax.rem(j, edge) * gcol, gcol), gcol),
        )

    def gram_start(ph, buf, recv):
        to_plane(ph, lambda j: buf.at[gspot(buf, j)], lambda i: recv.at[i])

    def gram_turn(ph, buf, recv, full):
        plane_wait(ph, recv).wait_recv()
        full[gspot(full, t)] = total(buf[gspot(buf, t)], recv).astype(BF)
        blk = full.at[gspot(full, t)]
        to_plane(ph + 1, lambda j: blk, lambda i: blk)

    @pl.when(p == 0)
    def _():
        def diagonal():
            shape = (own, LANES)
            return lax.broadcasted_iota(jnp.int32, shape, 0) == lax.broadcasted_iota(jnp.int32, shape, 1)

        def to_row(col):
            return jnp.sum(jnp.where(diagonal(), col, 0.0), axis=0, keepdims=True)

        def to_col(row):
            return jnp.sum(jnp.where(diagonal(), row, 0.0), axis=1, keepdims=True)

        def store_y(y, h):
            split(ybuf, y)
            hf = up(h)
            sq = jnp.sum(hf * hf, axis=1, keepdims=True)
            for i in range(2):
                tile = jnp.broadcast_to(to_row(sq[i * own : (i + 1) * own]), (8, LANES))
                for g in range(nt // 2):
                    ybuf[2 * g + i, own:] = tile

        def pick(b):
            g = t // 2
            out = b[0:1, :span]
            for i in range(1, nt // 2):
                out = jnp.where(g == i, b[0:1, i * span : (i + 1) * span], out)
            return out

        def norm(tot):
            return lax.rsqrt(to_col(tot[own : own + 1]) / width + 1e-05)

        def gate(tot, dc, inv, bound, buf):
            y = tot[:own]
            z = inv * y
            inside = (z >= -8.0 * bound) & (z <= 7.0 * bound)
            q = (inv * jnp.where(inside, dc, 0.0)).astype(BF)
            coef = to_row(inv * inv / width * jnp.sum(up(q) * y, axis=1, keepdims=True))
            hi = up(coef.astype(BF))
            row = lax.broadcasted_iota(jnp.int32, (16, LANES), 0)
            buf[t, :own] = q
            buf[t, own:] = jnp.where(row == 0, hi, jnp.where(row == 1, coef - hi, 0.0)).astype(BF)

        def coef_of(buf, i):
            ext = up(buf[i, own:])
            for g in range(1, nt // 2):
                ext = ext + up(buf[2 * g + i, own:])
            return to_col(jnp.sum(ext, axis=0, keepdims=True))

        def grad_in(buf, w):
            coef = jnp.concatenate([coef_of(buf, 0), coef_of(buf, 1)], axis=0)
            return dot_nt(join(buf), w), coef

        h0 = xall[d]
        store_y(dot(h0, v_ref[0]), h0)
        rs_start(1, ybuf, y0recv)
        share_inputs()
        plane_wait(13, pbrecv).wait_recv()
        pall[pl.ds(d, 1)] = total(pbuf[t // 2], pbrecv).astype(BF)[None]
        to_ring(3, lambda j: pall.at[d], lambda j: pall.at[d])
        tot0 = rs_total(1, ybuf, y0recv)
        inv0 = norm(tot0)
        bound0 = pick(bnd)
        cbuf[t] = jnp.clip(inv0 * tot0[:own], -8.0 * bound0, 7.0 * bound0).astype(BF)
        ag_start(2, cbuf)
        plane_wait(1, like(ybuf)).wait_send()
        dc1 = rs_total(0, dcbuf, dc1recv)
        e2 = rs_total(5, e2buf, e2recv)
        b1_copy.wait_recv()
        bound1 = pick(bnd1)
        ag_wait(2, cbuf)
        h1 = (up(xall[d]) + dot(join(cbuf), o_ref[0])).astype(BF)
        store_y(dot(h1, v1[...]), h1)
        rs_start(3, ybuf, y1recv)
        split(hobuf, dot_nt(h1, o_ref[0]))
        rs_start(14, hobuf, horecv)
        tot1 = rs_total(3, ybuf, y1recv)
        gate(tot1, dc1, norm(tot1), bound1, qbuf)
        ag_start(4, qbuf)
        ho = rs_total(14, hobuf, horecv)
        p_three = pall.at[pl.ds(0, nd - 1)]
        ring_wait(3, p_three).wait_recv()
        ag_wait(4, qbuf)
        q1 = side_of(qbuf, my_side)
        quarter = pall.shape[2]
        dc0 = e2 - coef_of(qbuf, my_side) * ho
        for i in range(nd):
            dc0 = dc0 + dot_nt(q1[:, i * quarter : (i + 1) * quarter], pall[i])
        gate(tot0, dc0, inv0, bound0, q0buf)
        ag_start(6, q0buf)
        lin, coef = grad_in(qbuf, v1[...])
        u1 = (up(u_ref[...]) + lin - coef * up(h1)).astype(BF)
        ag_wait(6, q0buf)
        lin, coef = grad_in(q0buf, v_ref[0])
        gall[pl.ds(d, 1)] = (up(u1) + lin - coef * up(xall[d])).astype(BF)[None]
        g_copy.start()
        for i in range(2):
            for k in (2, 1, 3):
                rcopy(gall.at[d], gall.at[d], gsend.at[i], grecv.at[i], (i, ring(k), t)).start()

    @pl.when(p == 1)
    def _():
        share_inputs()
        ring_wait(0, xall.at[pl.ds(0, nd - 1)]).wait_recv()
        xgram[0] = dot_nt(xall[d], xall[...].reshape(tokens, xall.shape[2])).astype(BF)
        gram_start(10, xgram, xgramrecv)
        gram_turn(10, xgram, xgramrecv, xgramall)
        plane_wait(11, xgramrecv).wait_recv()
        xx[...] = xgramall[0, pl.ds(mine, mine)]
        xx_copy.start()
        g_copy.wait_recv()

    vsum = dot_nt(rg[...].reshape(nd * rows, rg.shape[2]), gall[d]).astype(BF)
    vpart[...] = vsum.reshape(nd, rows, tg)
    vrow = rows // nt

    def vspot(j):
        return pl.ds(pl.multiple_of(j * vrow, vrow), vrow)

    to_plane(7, lambda j: vpart.at[:, vspot(j)], lambda i: vrecv.at[i])

    my_rows = pl.ds(pl.multiple_of(p * mine, mine), mine)
    g_three = gall.at[pl.ds(0, nd - 1)]

    @pl.when(p == 0)
    def _():
        ring_wait(0, xall.at[pl.ds(0, nd - 1)]).wait_recv()
        rcopy(g_three, g_three, gsend.at[0], grecv.at[0], partner).wait_recv()

    @pl.when(p == 1)
    def _():
        rcopy(g_three, g_three, gsend.at[1], grecv.at[1], partner).wait_recv()

    hid = xall[...].reshape(tokens, xall.shape[2])
    g_mine = gall[d, my_rows]
    x_mine = xall[d, my_rows]
    grad = gall[...].reshape(tokens, gall.shape[2])
    gram[0] = dot_nt(g_mine, hid).astype(BF)
    gram[1] = dot_nt(g_mine, grad).astype(BF)
    gram[2] = dot_nt(x_mine, grad).astype(BF)
    gram_start(8, gram, gramrecv)

    plane_wait(7, vrecv).wait_recv()
    vown[...] = total(vpart[:, vspot(t)], vrecv).astype(BF)
    vmine = (tz, ty, slice(None), pl.ds(pl.multiple_of(d * tg, tg), tg))

    def v_turn(step):
        cut = tokens // 2
        lo, hi = pl.ds(0, cut), pl.ds(cut, cut)
        if step == 0:
            along_y, along_z = vall.at[tz, ty, :, lo], vall.at[tz, ty, :, hi]
        else:
            along_y, along_z = vall.at[:, ty, :, hi], vall.at[tz, :, :, lo]
        for k in (2, 1, 3):
            to_y = (p, d, tz * edge + lax.rem(ty + k, edge))
            to_z = (p, d, lax.rem(tz + k, edge) * edge + ty)
            rcopy(along_y, along_y, vasend.at[step, 0], varecv.at[step, 0], to_y).start()
            rcopy(along_z, along_z, vasend.at[step, 1], varecv.at[step, 1], to_z).start()

    def v_waits(step):
        one = pl.ds(0, tokens // 2)
        blk = vall.at[0, pl.ds(0, edge - 1), :, one] if step == 0 else vall.at[pl.ds(0, edge - 1), :, :, one]
        return [rcopy(blk, blk, vasend.at[step, i], varecv.at[step, i], partner) for i in range(2)]

    to_ring(2, lambda j: vown.at[j], lambda j: vall.at[vmine])
    vall[vmine] = vown[d]

    gram_turn(8, gram, gramrecv, gramall)
    v_three = vown.at[pl.ds(0, nd - 1)]
    ring_wait(2, v_three).wait_recv()
    v_turn(0)

    e_three = eall.at[pl.ds(0, nd - 1)]
    ring_wait(1, e_three).wait_recv()
    emb_t = eall[...].reshape(tokens, rows).T

    @pl.when(p == 0)
    def _():
        xx_copy.wait_recv()

    for c in v_waits(0):
        c.wait_recv()
    v_turn(1)
    plane_wait(9, gramrecv).wait_recv()
    g_x, g_g, x_g, x_x = gramall[0], gramall[1], gramall[2], xx[...]

    def to_group(ph, src, dst):
        for k in (6, 2, 5, 7, 1, 3, 4):
            j = lax.rem(slot + k, group)
            rcopy(src, dst(k), gsend.at[ph], grecv.at[ph], (j // nd, lax.rem(j, nd), t)).start()

    def group_wait(ph, like):
        return rcopy(like, like, gsend.at[ph], grecv.at[ph], partner)

    nsbuf[...] = jnp.broadcast_to(8.0 * jnp.sum(up(x_x) * up(g_g) - up(g_x) * up(x_g)), nsbuf.shape)
    to_group(2, nsbuf, lambda k: nsrecv.at[k - 1])
    place = d * 2 + p

    def y_ring(k, to):
        blk = yall.at[lax.rem(d + to, nd) * 2 + p]
        return rcopy(blk, blk, ysend.at[k], yrecv.at[k], (p, ring(k), t))

    def y_chip(i):
        blk = yall.at[i]
        return rcopy(blk, blk, ysend.at[0], yrecv.at[0], partner)

    yall[place, 0] = (2.0 * (dot(g_x, grad) - dot(g_g, hid))).astype(BF)
    yall[place, 1] = (2.0 * (dot(x_g, hid) - dot(x_x, grad))).astype(BF)
    for k in (2, 1, 3):
        y_ring(k, 0).start()
    y_chip(place).start()

    for c in v_waits(1):
        c.wait_recv()
    vt = vall[...].reshape(rows, tokens)
    group_wait(2, nsrecv).wait_recv()
    ns = nsbuf[...]
    for k in range(group - 1):
        ns = ns + nsrecv[k]
    rate = jnp.sqrt(width / (ns[0:1, 0:1] + 1e-06))
    scale = math.sqrt(width)
    for k in (1, 3, 2):
        y_ring(k, nd - k).wait_recv()
        y_chip(lax.rem(d + nd - k, nd) * 2 + p).start()
    y_like = yall.at[pl.ds(0, nd)]
    y_all = rcopy(y_like, y_like, ysend.at[0], yrecv.at[0], partner)
    y_all.wait_recv()
    half_rate = -0.5 * rate
    za = (2.0 * up(grad) + half_rate * up(yall[:, 0].reshape(tokens, -1))).astype(BF)
    zb = (-2.0 * up(hid) + half_rate * up(yall[:, 1].reshape(tokens, -1))).astype(BF)
    cut = rows // 4
    for i in range(4):
        blk = slice(i * cut, (i + 1) * cut)
        last = dot(emb_t[blk], za) + dot(vt[blk], zb)
        out_ref[blk] = r_ref[blk] - (0.5 * scale) * rate * last

    for c in r_sends + r_on:
        c.wait_send()
    x_copy.wait_send()
    ring_wait(0, xall.at[pl.ds(0, nd - 1)]).wait_send()
    ring_wait(1, e_three).wait_send()
    ring_wait(2, v_three).wait_send()

    @pl.when(p == 0)
    def _():
        plane_wait(0, like(dcbuf)).wait_send()
        plane_wait(2, like(cbuf)).wait_send()
        plane_wait(3, like(ybuf)).wait_send()
        plane_wait(4, like(qbuf)).wait_send()
        plane_wait(5, like(e2buf)).wait_send()
        plane_wait(6, like(q0buf)).wait_send()
        plane_wait(13, pbrecv).wait_send()
        plane_wait(14, like(hobuf)).wait_send()
        ring_wait(3, pall.at[pl.ds(0, nd - 1)]).wait_send()
        g_copy.wait_send()
        rcopy(g_three, g_three, gsend.at[0], grecv.at[0], partner).wait_send()
        rcopy(g_three, g_three, gsend.at[1], grecv.at[1], partner).wait_send()

    @pl.when(p == 1)
    def _():
        d1_copy.wait_send()
        b1_copy.wait_send()
        v1_copy.wait_send()
        plane_wait(10, xgramrecv).wait_send()
        plane_wait(11, xgramrecv).wait_send()
        xx_copy.wait_send()

    plane_wait(7, vrecv).wait_send()
    plane_wait(8, gramrecv).wait_send()
    plane_wait(9, gramrecv).wait_send()
    for step in range(2):
        for c in v_waits(step):
            c.wait_send()
    group_wait(2, nsrecv).wait_send()
    for k in (1, 2, 3):
        y_ring(k, 0).wait_send()
    y_all.wait_send()


def solution(mesh):
    nd = mesh.shape["dp"]
    nt = mesh.shape["tensor"]

    def local(embedded, rotation, value_proj, output_proj, mid_exponent, cotangent):
        tg = embedded.shape[0]
        rows, cols = rotation.shape
        width = cols * nt
        units = value_proj.shape[2]
        own = tg // 2
        span = units // (nt // 2)
        group = 2 * nd
        edge = math.isqrt(nt)
        mine = tg // 2
        tokens = nd * tg
        vm = pltpu.VMEM
        dma = pltpu.SemaphoreType.DMA
        scratch = [
            vm(embedded.shape, BF),
            vm(rotation.shape, F32),
            vm(value_proj.shape, BF),
            vm(output_proj.shape, BF),
            vm(mid_exponent.shape, jnp.int32),
            vm(cotangent.shape, BF),
            vm((nd, rows, cols), BF),
            vm((tg, cols), BF),
            vm((tg, cols), BF),
            vm((nd, tg, cols), BF),
            vm((nd, tg, rows), BF),
            vm((nd, tg, cols), BF),
            vm((cols, units), BF),
            vm((8, units), F32),
            vm((8, units), F32),
            vm((nt, own, span), BF),
            vm((nt - 1, own, span), BF),
            vm((nt, own, span), BF),
            vm((nt - 1, own, span), BF),
            vm((nt, own, span), BF),
            vm((nt - 1, own, span), BF),
            vm((nt // 2, span, units // nd), BF),
            vm((nt - 1, span, units // nd), BF),
            vm((nd, span, units // nd), BF),
            vm((nt, own + 8, span), YT),
            vm((nt - 1, own + 8, span), YT),
            vm((nt - 1, own + 8, span), YT),
            vm((nt, own, span), BF),
            vm((nt, own + 16, span), BF),
            vm((nt, own + 16, span), BF),
            vm((nd, rows, tg), BF),
            vm((nt - 1, nd, rows // nt, tg), BF),
            vm((nd, rows // nt, tg), BF),
            vm((edge, edge, rows // nt, tokens), BF),
            vm((3, mine, tokens), BF),
            vm((nt - 1, 3, mine // edge, tokens // edge), BF),
            vm((3, mine, tokens), BF),
            vm((1, tg, tokens), BF),
            vm((nt - 1, 1, tg // edge, tokens // edge), BF),
            vm((1, tg, tokens), BF),
            vm((mine, tokens), BF),
            vm((group, 2, mine, cols), BF),
            vm((8, LANES), F32),
            vm((group - 1, 8, LANES), F32),
            dma((6,)),
            dma((15,)),
            dma((15,)),
            dma((12,)),
            dma((12,)),
            dma((4,)),
            dma((4,)),
            dma((3,)),
            dma((3,)),
            dma((6,)),
            dma((6,)),
            dma((nd,)),
            dma((nd,)),
            dma((2, 2)),
            dma((2, 2)),
        ]
        step = pl.pallas_call(
            functools.partial(kernel, nd, nt, float(width)),
            out_shape=pltpu.VMEM((rows, cols), OT),
            in_specs=[pl.BlockSpec(memory_space=pltpu.HBM)] * 6,
            out_specs=pl.BlockSpec(memory_space=pltpu.VMEM),
            scratch_shapes=scratch,
            compiler_params=pltpu.CompilerParams(
                collective_id=0, has_side_effects=True, vmem_limit_bytes=60000000
            ),
        )(*[pltpu.with_memory_space_constraint(x, pltpu.HBM) for x in (embedded, rotation, value_proj, output_proj, mid_exponent, cotangent)])
        return step

    return jax.shard_map(
        local,
        mesh=mesh,
        in_specs=(
            P("dp", "pipe"),
            P(("pipe", "dp"), "tensor"),
            P("pipe", "tensor", None),
            P("pipe", None, "tensor"),
            P("pipe", None),
            P("dp", "tensor"),
        ),
        out_specs=P(("pipe", "dp"), "tensor"),
        check_vma=False,
    )
```

```python
import functools
import math

import jax
import jax.numpy as jnp
from jax import lax
from jax.experimental import pallas as pl
from jax.experimental.pallas import tpu as pltpu
from jax.sharding import PartitionSpec as P

BF = jnp.bfloat16
F32 = jnp.float32
YT = jnp.float32
OT = jnp.float32
LANES = 128
NT_DIMS = (((1,), (1,)), ((), ()))


def dot(a, b):
    return jnp.dot(a, b, preferred_element_type=F32)


def dot_nt(a, b):
    return lax.dot_general(a, b, NT_DIMS, preferred_element_type=F32)


def up(a):
    return a.astype(F32)


def far_first(edge):
    cells = [(a, b) for a in range(edge) for b in range(edge) if a or b]
    return sorted(cells, key=lambda c: -min(c[0], edge - c[0]) - min(c[1], edge - c[1]))


def kernel(
    nd,
    nt,
    width,
    e_hbm,
    r_hbm,
    v_hbm,
    o_hbm,
    m_hbm,
    u_hbm,
    out_ref,
    e_ref,
    r_ref,
    v_ref,
    o_ref,
    m_ref,
    u_ref,
    rg,
    xpart,
    xrecv,
    xall,
    eall,
    gall,
    v1,
    bnd,
    bnd1,
    dcbuf,
    dc1recv,
    e2buf,
    e2recv,
    hobuf,
    horecv,
    pbuf,
    pbrecv,
    pall,
    ybuf,
    y0recv,
    y1recv,
    cbuf,
    qbuf,
    q0buf,
    vpart,
    vrecv,
    vown,
    vall,
    gram,
    gramrecv,
    gramall,
    xgram,
    xgramrecv,
    xgramall,
    xx,
    yall,
    nsbuf,
    nsrecv,
    embt,
    insem,
    tsend,
    trecv,
    rsend,
    rrecv,
    xsend,
    xrecv_sem,
    gsend,
    grecv,
    psend,
    precv,
    ysend,
    yrecv,
    vasend,
    varecv,
):
    p = lax.axis_index("pipe")
    d = lax.axis_index("dp")
    t = lax.axis_index("tensor")
    tg = u_ref.shape[0]
    span = ybuf.shape[2]
    own = tg // 2
    rows = rg.shape[1]
    group = 2 * nd
    slot = p * nd + d
    edge = math.isqrt(nt)
    tz, ty = t // edge, lax.rem(t, edge)
    tokens = nd * tg
    mine = tg // 2
    pair = edge // 2

    def rcopy(src, dst, ssem, rsem, to):
        return pltpu.make_async_remote_copy(
            src_ref=src,
            dst_ref=dst,
            send_sem=ssem,
            recv_sem=rsem,
            device_id=to,
            device_id_type=pl.DeviceIdType.MESH,
        )

    others = []
    for a, b in far_first(edge):
        others.append(lax.rem(tz + a, edge) * edge + lax.rem(ty + b, edge))

    def to_plane(ph, src, dst):
        for i, j in enumerate(others):
            rcopy(src(j), dst(i), tsend.at[ph], trecv.at[ph], (p, d, j)).start()

    def plane_wait(ph, like):
        return rcopy(like, like, tsend.at[ph], trecv.at[ph], (p, d, others[-1]))

    def total(first, recv):
        acc = first.astype(F32)
        for i in range(nt - 1):
            acc = acc + recv[i].astype(F32)
        return acc

    def piece(i, g):
        return (g // pair) * edge + i * pair + g % pair

    def side(j):
        return lax.rem(j, edge) // pair

    def unit_group(j):
        return (j // edge) * pair + lax.rem(lax.rem(j, edge), pair)

    my_side = side(t)

    def split(buf, y):
        for i in range(2):
            for g in range(nt // 2):
                blk = y[i * own : (i + 1) * own, g * span : (g + 1) * span]
                buf[piece(i, g), :own] = blk.astype(buf.dtype)

    def side_of(buf, i):
        return jnp.concatenate([buf[piece(i, g), :own] for g in range(nt // 2)], axis=1)

    def join(buf):
        return jnp.concatenate([side_of(buf, 0), side_of(buf, 1)], axis=0)

    def like(buf):
        return buf.at[pl.ds(0, nt - 1)]

    def rs_start(ph, buf, recv):
        to_plane(ph, lambda j: buf.at[j], lambda i: recv.at[i])

    def rs_total(ph, buf, recv):
        plane_wait(ph, recv).wait_recv()
        return total(buf[t], recv)

    def ag_start(ph, buf):
        to_plane(ph, lambda j: buf.at[t], lambda i: buf.at[t])

    def ag_wait(ph, buf):
        plane_wait(ph, like(buf)).wait_recv()

    def ring(k):
        return lax.rem(d + k, nd)

    partner = (1 - p, d, t)

    def to_ring(ph, src, dst):
        for k in (2, 1, 3):
            rcopy(src(ring(k)), dst(ring(k)), xsend.at[ph], xrecv_sem.at[ph], (p, ring(k), t)).start()

    def ring_wait(ph, like):
        return rcopy(like, like, xsend.at[ph], xrecv_sem.at[ph], (p, ring(1), t))

    loads = [
        pltpu.make_async_copy(src, dst, insem.at[i])
        for i, (src, dst) in enumerate(
            (
                (r_hbm, r_ref),
                (u_hbm, u_ref),
                (o_hbm, o_ref),
                (m_hbm, m_ref),
                (v_hbm, v_ref),
                (e_hbm, e_ref),
            )
        )
    ]
    loads[0].start()

    bar = pltpu.get_barrier_semaphore()

    def greet(to):
        pl.semaphore_signal(bar, inc=1, device_id=to, device_id_type=pl.DeviceIdType.MESH)

    for j in others:
        greet((p, d, j))
    for k in range(1, nd):
        greet((p, ring(k), t))
        greet((1 - p, ring(k), t))
    greet(partner)

    loads[0].wait()
    for load in loads[1:]:
        load.start()
    rg[pl.ds(d, 1)] = (r_ref[...] * (1.0 / math.sqrt(width))).astype(BF)[None]
    pl.semaphore_wait(bar, nt - 1 + 2 * (nd - 1) + 1)

    hrow = rows // 2

    def r_half(s, h, to, i):
        blk = rg.at[s, pl.ds(h * hrow, hrow)]
        return rcopy(blk, blk, rsend.at[i], rrecv.at[i], (p, ring(to), t))

    ahead, behind = 1, nd - 1
    r_sends = [
        r_half(d, 0, ahead, 0),
        r_half(d, 1, behind, 1),
        r_half(d, 1, ahead, 2),
        r_half(d, 0, behind, 3),
    ]
    r_gets = [
        r_half(ring(behind), 0, ahead, 0),
        r_half(ring(ahead), 1, behind, 1),
        r_half(ring(behind), 1, ahead, 2),
        r_half(ring(ahead), 0, behind, 3),
    ]
    r_on = [r_half(ring(behind), 0, ahead, 4), r_half(ring(ahead), 1, behind, 5)]
    r_far = [r_half(ring(2), 0, ahead, 4), r_half(ring(2), 1, behind, 5)]
    for c in r_sends:
        c.start()
    for load in loads[1:]:
        load.wait()

    v1_copy = rcopy(v_ref.at[0], v1, psend.at[0], precv.at[0], partner)
    b1_copy = rcopy(bnd, bnd1, psend.at[1], precv.at[1], partner)
    d1_copy = rcopy(dcbuf, dcbuf, psend.at[2], precv.at[2], partner)
    x_copy = rcopy(xpart, xrecv, psend.at[3], precv.at[3], partner)
    xx_copy = rcopy(xgramall.at[0, pl.ds(0, mine)], xx, psend.at[4], precv.at[4], partner)
    g_copy = rcopy(gall.at[d], gall.at[d], psend.at[5], precv.at[5], partner)

    bnd[...] = jnp.broadcast_to(jnp.exp2(m_ref[...].astype(F32)), bnd.shape)

    @pl.when(p == 1)
    def _():
        v1_copy.start()
        split(dcbuf, dot_nt(u_ref[...], o_ref[0]))
        d1_copy.start()
        b1_copy.start()

    @pl.when(p == 0)
    def _():
        split(e2buf, dot_nt(u_ref[...], o_ref[0]))
        v1_copy.wait_recv()
        quarter = pbuf.shape[2]
        cross = dot(o_ref[0], v1[:, pl.ds(pl.multiple_of(d * quarter, quarter), quarter)])
        pbuf[...] = cross.astype(BF).reshape(pbuf.shape)
        to_plane(13, lambda j: pbuf.at[unit_group(j)], lambda i: pbrecv.at[i])
        rs_start(5, e2buf, e2recv)
        d1_copy.wait_recv()
        rs_start(0, dcbuf, dc1recv)

    def e_dot(s):
        return dot(e_ref[:, pl.ds(pl.multiple_of(s * rows, LANES), rows)], rg[s])

    r_gets[0].wait_recv()
    r_on[0].start()
    r_gets[1].wait_recv()
    r_on[1].start()
    part = e_dot(d)
    r_gets[2].wait_recv()
    r_gets[3].wait_recv()
    part = part + e_dot(ring(1)) + e_dot(ring(3))
    r_far[0].wait_recv()
    r_far[1].wait_recv()
    part = part + e_dot(ring(2))
    xpart[...] = part.astype(BF)
    x_copy.start()
    x_copy.wait_recv()
    xall[pl.ds(d, 1)] = (up(xpart[...]) + up(xrecv[...])).astype(BF)[None]

    def share_inputs():
        to_ring(0, lambda j: xall.at[d], lambda j: xall.at[d])
        to_ring(
            1,
            lambda j: e_ref.at[:, pl.ds(pl.multiple_of(j * rows, LANES), rows)],
            lambda j: eall.at[d],
        )
        eall[pl.ds(d, 1)] = e_ref[:, pl.ds(pl.multiple_of(d * rows, LANES), rows)][None]

    gcol = tokens // edge

    def gspot(buf, j):
        grow = buf.shape[1] // edge
        return (
            slice(None),
            pl.ds(pl.multiple_of((j // edge) * grow, grow), grow),
            pl.ds(pl.multiple_of(lax.rem(j, edge) * gcol, gcol), gcol),
        )

    def gram_start(ph, buf, recv):
        to_plane(ph, lambda j: buf.at[gspot(buf, j)], lambda i: recv.at[i])

    def gram_turn(ph, buf, recv, full):
        plane_wait(ph, recv).wait_recv()
        full[gspot(full, t)] = total(buf[gspot(buf, t)], recv).astype(BF)
        blk = full.at[gspot(full, t)]
        to_plane(ph + 1, lambda j: blk, lambda i: blk)

    @pl.when(p == 0)
    def _():
        def diagonal():
            shape = (own, LANES)
            return lax.broadcasted_iota(jnp.int32, shape, 0) == lax.broadcasted_iota(jnp.int32, shape, 1)

        def to_row(col):
            return jnp.sum(jnp.where(diagonal(), col, 0.0), axis=0, keepdims=True)

        def to_col(row):
            return jnp.sum(jnp.where(diagonal(), row, 0.0), axis=1, keepdims=True)

        def store_y(y, h):
            split(ybuf, y)
            hf = up(h)
            sq = jnp.sum(hf * hf, axis=1, keepdims=True)
            for i in range(2):
                tile = jnp.broadcast_to(to_row(sq[i * own : (i + 1) * own]), (8, LANES))
                for g in range(nt // 2):
                    ybuf[piece(i, g), own:] = tile

        def pick(b):
            g = unit_group(t)
            out = b[0:1, :span]
            for i in range(1, nt // 2):
                out = jnp.where(g == i, b[0:1, i * span : (i + 1) * span], out)
            return out

        def norm(tot):
            return lax.rsqrt(to_col(tot[own : own + 1]) / width + 1e-05)

        def gate(tot, dc, inv, bound, buf):
            y = tot[:own]
            z = inv * y
            inside = (z >= -8.0 * bound) & (z <= 7.0 * bound)
            q = (inv * jnp.where(inside, dc, 0.0)).astype(BF)
            coef = to_row(inv * inv / width * jnp.sum(up(q) * y, axis=1, keepdims=True))
            hi = up(coef.astype(BF))
            row = lax.broadcasted_iota(jnp.int32, (16, LANES), 0)
            buf[t, :own] = q
            buf[t, own:] = jnp.where(row == 0, hi, jnp.where(row == 1, coef - hi, 0.0)).astype(BF)

        def coef_of(buf, i):
            ext = up(buf[piece(i, 0), own:])
            for g in range(1, nt // 2):
                ext = ext + up(buf[piece(i, g), own:])
            return to_col(jnp.sum(ext, axis=0, keepdims=True))

        def grad_in(buf, w):
            coef = jnp.concatenate([coef_of(buf, 0), coef_of(buf, 1)], axis=0)
            return dot_nt(join(buf), w), coef

        h0 = xall[d]
        store_y(dot(h0, v_ref[0]), h0)
        rs_start(1, ybuf, y0recv)
        share_inputs()
        plane_wait(13, pbrecv).wait_recv()
        pall[pl.ds(d, 1)] = total(pbuf[unit_group(t)], pbrecv).astype(BF)[None]
        to_ring(3, lambda j: pall.at[d], lambda j: pall.at[d])
        tot0 = rs_total(1, ybuf, y0recv)
        inv0 = norm(tot0)
        bound0 = pick(bnd)
        cbuf[t] = jnp.clip(inv0 * tot0[:own], -8.0 * bound0, 7.0 * bound0).astype(BF)
        ag_start(2, cbuf)
        plane_wait(1, like(ybuf)).wait_send()
        dc1 = rs_total(0, dcbuf, dc1recv)
        e2 = rs_total(5, e2buf, e2recv)
        b1_copy.wait_recv()
        bound1 = pick(bnd1)
        ag_wait(2, cbuf)
        h1 = (up(xall[d]) + dot(join(cbuf), o_ref[0])).astype(BF)
        store_y(dot(h1, v1[...]), h1)
        rs_start(3, ybuf, y1recv)
        split(hobuf, dot_nt(h1, o_ref[0]))
        rs_start(14, hobuf, horecv)
        tot1 = rs_total(3, ybuf, y1recv)
        gate(tot1, dc1, norm(tot1), bound1, qbuf)
        mates, rest = [], []
        for a in (2, 1, 3, 0):
            row = lax.rem(tz + a, edge) * edge
            for c in range(pair - 1, -1, -1):
                if a or c:
                    mates.append(row + my_side * pair + lax.rem(ty + c, pair))
                rest.append(row + (1 - my_side) * pair + lax.rem(ty + c, pair))
        for ph, targets in ((4, mates), (15, rest)):
            for j in targets:
                rcopy(qbuf.at[t], qbuf.at[t], tsend.at[ph], trecv.at[ph], (p, d, j)).start()
        q_mates = plane_wait(4, qbuf.at[pl.ds(0, nt // 2 - 1)])
        q_rest = plane_wait(15, qbuf.at[pl.ds(0, nt // 2)])
        ho = rs_total(14, hobuf, horecv)
        p_three = pall.at[pl.ds(0, nd - 1)]
        ring_wait(3, p_three).wait_recv()
        q_mates.wait_recv()
        q1 = side_of(qbuf, my_side)
        quarter = pall.shape[2]
        dc0 = e2 - coef_of(qbuf, my_side) * ho
        for i in range(nd):
            dc0 = dc0 + dot_nt(q1[:, i * quarter : (i + 1) * quarter], pall[i])
        gate(tot0, dc0, inv0, bound0, q0buf)
        ag_start(6, q0buf)
        q_rest.wait_recv()
        lin, coef = grad_in(qbuf, v1[...])
        u1 = (up(u_ref[...]) + lin - coef * up(h1)).astype(BF)
        ag_wait(6, q0buf)
        lin, coef = grad_in(q0buf, v_ref[0])
        gall[pl.ds(d, 1)] = (up(u1) + lin - coef * up(xall[d])).astype(BF)[None]
        g_copy.start()
        for i in range(2):
            for k in (2, 1, 3):
                rcopy(gall.at[d], gall.at[d], gsend.at[i], grecv.at[i], (i, ring(k), t)).start()

    @pl.when(p == 1)
    def _():
        share_inputs()
        ring_wait(0, xall.at[pl.ds(0, nd - 1)]).wait_recv()
        pair = pl.ds(pl.multiple_of(lax.rem(d, 2) * mine, mine), mine)
        both = jnp.concatenate([xall[i * (nd // 2) + d // 2, pair] for i in range(2)], axis=0)
        xgram[0] = dot_nt(both, xall[...].reshape(tokens, xall.shape[2])).astype(BF)
        gram_start(10, xgram, xgramrecv)
        gram_turn(10, xgram, xgramrecv, xgramall)
        plane_wait(11, xgramrecv).wait_recv()
        xx[...] = xgramall[0, pl.ds(mine, mine)]
        xx_copy.start()
        g_copy.wait_recv()

    vsum = dot_nt(rg[...].reshape(nd * rows, rg.shape[2]), gall[d]).astype(BF)
    vpart[...] = vsum.reshape(nd, rows, tg)
    vrow = rows // nt

    def vspot(j):
        return pl.ds(pl.multiple_of(j * vrow, vrow), vrow)

    to_plane(7, lambda j: vpart.at[:, vspot(j)], lambda i: vrecv.at[i])

    my_group = p * (nd // 2) + d // 2
    my_rows = pl.ds(pl.multiple_of(lax.rem(d, 2) * mine, mine), mine)
    g_three = gall.at[pl.ds(0, nd - 1)]

    @pl.when(p == 0)
    def _():
        ring_wait(0, xall.at[pl.ds(0, nd - 1)]).wait_recv()
        rcopy(g_three, g_three, gsend.at[0], grecv.at[0], partner).wait_recv()

    @pl.when(p == 1)
    def _():
        rcopy(g_three, g_three, gsend.at[1], grecv.at[1], partner).wait_recv()

    hid = xall[...].reshape(tokens, xall.shape[2])
    g_mine = gall[my_group, my_rows]
    x_mine = xall[my_group, my_rows]
    grad = gall[...].reshape(tokens, gall.shape[2])
    gram[0] = dot_nt(g_mine, hid).astype(BF)
    gram[1] = dot_nt(g_mine, grad).astype(BF)
    gram[2] = dot_nt(x_mine, grad).astype(BF)
    gram_start(8, gram, gramrecv)

    plane_wait(7, vrecv).wait_recv()
    vown[...] = total(vpart[:, vspot(t)], vrecv).astype(BF)
    vmine = (tz, ty, slice(None), pl.ds(pl.multiple_of(d * tg, tg), tg))

    def v_turn(step):
        cut = tokens // 2
        lo, hi = pl.ds(0, cut), pl.ds(cut, cut)
        if step == 0:
            along_y, along_z = vall.at[tz, ty, :, lo], vall.at[tz, ty, :, hi]
        else:
            along_y, along_z = vall.at[:, ty, :, hi], vall.at[tz, :, :, lo]
        for k in (2, 1, 3):
            to_y = (p, d, tz * edge + lax.rem(ty + k, edge))
            to_z = (p, d, lax.rem(tz + k, edge) * edge + ty)
            rcopy(along_y, along_y, vasend.at[step, 0], varecv.at[step, 0], to_y).start()
            rcopy(along_z, along_z, vasend.at[step, 1], varecv.at[step, 1], to_z).start()

    def v_waits(step):
        one = pl.ds(0, tokens // 2)
        blk = vall.at[0, pl.ds(0, edge - 1), :, one] if step == 0 else vall.at[pl.ds(0, edge - 1), :, :, one]
        return [rcopy(blk, blk, vasend.at[step, i], varecv.at[step, i], partner) for i in range(2)]

    to_ring(2, lambda j: vown.at[j], lambda j: vall.at[vmine])
    vall[vmine] = vown[d]

    gram_turn(8, gram, gramrecv, gramall)
    v_three = vown.at[pl.ds(0, nd - 1)]
    ring_wait(2, v_three).wait_recv()
    v_turn(0)

    e_three = eall.at[pl.ds(0, nd - 1)]
    ring_wait(1, e_three).wait_recv()
    embt[...] = eall[...].reshape(tokens, rows).T

    @pl.when(p == 0)
    def _():
        xx_copy.wait_recv()

    for c in v_waits(0):
        c.wait_recv()
    v_turn(1)
    plane_wait(9, gramrecv).wait_recv()
    g_x, g_g, x_g, x_x = gramall[0], gramall[1], gramall[2], xx[...]

    def to_group(ph, src, dst):
        for k in (6, 2, 5, 7, 1, 3, 4):
            j = lax.rem(slot + k, group)
            rcopy(src, dst(k), gsend.at[ph], grecv.at[ph], (j // nd, lax.rem(j, nd), t)).start()

    def group_wait(ph, like):
        return rcopy(like, like, gsend.at[ph], grecv.at[ph], partner)

    nsbuf[...] = jnp.broadcast_to(8.0 * jnp.sum(up(x_x) * up(g_g) - up(g_x) * up(x_g)), nsbuf.shape)
    to_group(2, nsbuf, lambda k: nsrecv.at[k - 1])
    place = slot

    def y_ring(k, to):
        blk = yall.at[p * nd + lax.rem(d + to, nd)]
        return rcopy(blk, blk, ysend.at[k], yrecv.at[k], (p, ring(k), t))

    def y_chip(i):
        blk = yall.at[i]
        return rcopy(blk, blk, ysend.at[0], yrecv.at[0], partner)

    yall[place, 0] = (2.0 * (dot(g_x, grad) - dot(g_g, hid))).astype(BF)
    yall[place, 1] = (2.0 * (dot(x_g, hid) - dot(x_x, grad))).astype(BF)
    for k in (2, 1, 3):
        y_ring(k, 0).start()
    y_chip(place).start()

    for c in v_waits(1):
        c.wait_recv()

    def vt_of(lanes):
        return vall[:, :, :, lanes].reshape(rows, tokens // 2)

    group_wait(2, nsrecv).wait_recv()
    ns = nsbuf[...]
    for k in range(group - 1):
        ns = ns + nsrecv[k]
    rate = jnp.sqrt(width / (ns[0:1, 0:1] + 1e-06))
    scale = math.sqrt(width)
    for k in (1, 3, 2):
        y_ring(k, nd - k).wait_recv()
        y_chip(p * nd + lax.rem(d + nd - k, nd)).start()
    y_like = yall.at[pl.ds(0, nd)]
    y_all = rcopy(y_like, y_like, ysend.at[0], yrecv.at[0], partner)

    cut = tokens // 2

    def part_of(i):
        pieces = yall[pl.ds(i * nd, nd)]
        groups = pl.ds(i * (nd // 2), nd // 2)
        za = 2.0 * up(gall[groups].reshape(cut, -1)) - 0.5 * rate * up(pieces[:, 0].reshape(cut, -1))
        zb = -2.0 * up(xall[groups].reshape(cut, -1)) - 0.5 * rate * up(pieces[:, 1].reshape(cut, -1))
        lanes = pl.ds(pl.multiple_of(i * cut, cut), cut)
        return dot(embt[:, lanes], za.astype(BF)) + dot(vt_of(lanes), zb.astype(BF))

    out_ref[...] = r_ref[...] - (0.5 * scale) * rate * part_of(p)
    y_all.wait_recv()
    out_ref[...] = out_ref[...] - (0.5 * scale) * rate * part_of(1 - p)

    for c in r_sends + r_on:
        c.wait_send()
    x_copy.wait_send()
    ring_wait(0, xall.at[pl.ds(0, nd - 1)]).wait_send()
    ring_wait(1, e_three).wait_send()
    ring_wait(2, v_three).wait_send()

    @pl.when(p == 0)
    def _():
        plane_wait(0, like(dcbuf)).wait_send()
        plane_wait(2, like(cbuf)).wait_send()
        plane_wait(3, like(ybuf)).wait_send()
        plane_wait(4, qbuf.at[pl.ds(0, nt // 2 - 1)]).wait_send()
        plane_wait(15, qbuf.at[pl.ds(0, nt // 2)]).wait_send()
        plane_wait(5, like(e2buf)).wait_send()
        plane_wait(6, like(q0buf)).wait_send()
        plane_wait(13, pbrecv).wait_send()
        plane_wait(14, like(hobuf)).wait_send()
        ring_wait(3, pall.at[pl.ds(0, nd - 1)]).wait_send()
        g_copy.wait_send()
        rcopy(g_three, g_three, gsend.at[0], grecv.at[0], partner).wait_send()
        rcopy(g_three, g_three, gsend.at[1], grecv.at[1], partner).wait_send()

    @pl.when(p == 1)
    def _():
        d1_copy.wait_send()
        b1_copy.wait_send()
        v1_copy.wait_send()
        plane_wait(10, xgramrecv).wait_send()
        plane_wait(11, xgramrecv).wait_send()
        xx_copy.wait_send()

    plane_wait(7, vrecv).wait_send()
    plane_wait(8, gramrecv).wait_send()
    plane_wait(9, gramrecv).wait_send()
    for step in range(2):
        for c in v_waits(step):
            c.wait_send()
    group_wait(2, nsrecv).wait_send()
    for k in (1, 2, 3):
        y_ring(k, 0).wait_send()
    y_all.wait_send()


def solution(mesh):
    nd = mesh.shape["dp"]
    nt = mesh.shape["tensor"]

    def local(embedded, rotation, value_proj, output_proj, mid_exponent, cotangent):
        tg = embedded.shape[0]
        rows, cols = rotation.shape
        width = cols * nt
        units = value_proj.shape[2]
        own = tg // 2
        span = units // (nt // 2)
        group = 2 * nd
        edge = math.isqrt(nt)
        mine = tg // 2
        tokens = nd * tg
        vm = pltpu.VMEM
        dma = pltpu.SemaphoreType.DMA
        scratch = [
            vm(embedded.shape, BF),
            vm(rotation.shape, F32),
            vm(value_proj.shape, BF),
            vm(output_proj.shape, BF),
            vm(mid_exponent.shape, jnp.int32),
            vm(cotangent.shape, BF),
            vm((nd, rows, cols), BF),
            vm((tg, cols), BF),
            vm((tg, cols), BF),
            vm((nd, tg, cols), BF),
            vm((nd, tg, rows), BF),
            vm((nd, tg, cols), BF),
            vm((cols, units), BF),
            vm((8, units), F32),
            vm((8, units), F32),
            vm((nt, own, span), BF),
            vm((nt - 1, own, span), BF),
            vm((nt, own, span), BF),
            vm((nt - 1, own, span), BF),
            vm((nt, own, span), BF),
            vm((nt - 1, own, span), BF),
            vm((nt // 2, span, units // nd), BF),
            vm((nt - 1, span, units // nd), BF),
            vm((nd, span, units // nd), BF),
            vm((nt, own + 8, span), YT),
            vm((nt - 1, own + 8, span), YT),
            vm((nt - 1, own + 8, span), YT),
            vm((nt, own, span), BF),
            vm((nt, own + 16, span), BF),
            vm((nt, own + 16, span), BF),
            vm((nd, rows, tg), BF),
            vm((nt - 1, nd, rows // nt, tg), BF),
            vm((nd, rows // nt, tg), BF),
            vm((edge, edge, rows // nt, tokens), BF),
            vm((3, mine, tokens), BF),
            vm((nt - 1, 3, mine // edge, tokens // edge), BF),
            vm((3, mine, tokens), BF),
            vm((1, tg, tokens), BF),
            vm((nt - 1, 1, tg // edge, tokens // edge), BF),
            vm((1, tg, tokens), BF),
            vm((mine, tokens), BF),
            vm((group, 2, mine, cols), BF),
            vm((8, LANES), F32),
            vm((group - 1, 8, LANES), F32),
            vm((rows, tokens), BF),
            dma((6,)),
            dma((16,)),
            dma((16,)),
            dma((12,)),
            dma((12,)),
            dma((4,)),
            dma((4,)),
            dma((3,)),
            dma((3,)),
            dma((6,)),
            dma((6,)),
            dma((nd,)),
            dma((nd,)),
            dma((2, 2)),
            dma((2, 2)),
        ]
        step = pl.pallas_call(
            functools.partial(kernel, nd, nt, float(width)),
            out_shape=pltpu.VMEM((rows, cols), OT),
            in_specs=[pl.BlockSpec(memory_space=pltpu.HBM)] * 6,
            out_specs=pl.BlockSpec(memory_space=pltpu.VMEM),
            scratch_shapes=scratch,
            compiler_params=pltpu.CompilerParams(
                collective_id=0, has_side_effects=True, vmem_limit_bytes=60000000
            ),
        )(*[pltpu.with_memory_space_constraint(x, pltpu.HBM) for x in (embedded, rotation, value_proj, output_proj, mid_exponent, cotangent)])
        return step

    return jax.shard_map(
        local,
        mesh=mesh,
        in_specs=(
            P("dp", "pipe"),
            P(("pipe", "dp"), "tensor"),
            P("pipe", "tensor", None),
            P("pipe", None, "tensor"),
            P("pipe", None),
            P("dp", "tensor"),
        ),
        out_specs=P(("pipe", "dp"), "tensor"),
        check_vma=False,
    )
```

```python
import functools
import math

import jax
import jax.numpy as jnp
from jax import lax
from jax.experimental import pallas as pl
from jax.experimental.pallas import tpu as pltpu
from jax.sharding import PartitionSpec as P

BF = jnp.bfloat16
F32 = jnp.float32
YT = jnp.float32
OT = jnp.float32
LANES = 128
NT_DIMS = (((1,), (1,)), ((), ()))


def dot(a, b):
    return jnp.dot(a, b, preferred_element_type=F32)


def dot_nt(a, b):
    return lax.dot_general(a, b, NT_DIMS, preferred_element_type=F32)


def up(a):
    return a.astype(F32)


def far_first(edge):
    cells = [(a, b) for a in range(edge) for b in range(edge) if a or b]
    hops = [[min(x, edge - x) for x in c] for c in cells]
    return [c for _, c in sorted(zip(hops, cells), key=lambda h: (-sum(h[0]), -h[0][0] if sum(h[0]) > 1 else h[0][0]))]


def kernel(
    nd,
    nt,
    width,
    e_hbm,
    r_hbm,
    v_hbm,
    o_hbm,
    m_hbm,
    u_hbm,
    out_ref,
    e_ref,
    r_ref,
    v_ref,
    o_ref,
    m_ref,
    u_ref,
    rg,
    xpart,
    xrecv,
    xall,
    eall,
    gall,
    v1,
    bnd,
    bnd1,
    dcbuf,
    dc1recv,
    e2buf,
    e2recv,
    hobuf,
    horecv,
    pbuf,
    pbrecv,
    pall,
    ybuf,
    y0recv,
    y1recv,
    cbuf,
    qbuf,
    q0buf,
    vpart,
    vrecv,
    vown,
    vall,
    gram,
    gramrecv,
    gramall,
    xgram,
    xgramrecv,
    xgramall,
    xx,
    yall,
    nsbuf,
    nsrecv,
    embt,
    insem,
    tsend,
    trecv,
    rsend,
    rrecv,
    xsend,
    xrecv_sem,
    gsend,
    grecv,
    psend,
    precv,
    ysend,
    yrecv,
    vasend,
    varecv,
):
    p = lax.axis_index("pipe")
    d = lax.axis_index("dp")
    t = lax.axis_index("tensor")
    tg = u_ref.shape[0]
    span = ybuf.shape[2]
    own = tg // 2
    rows = rg.shape[1]
    group = 2 * nd
    slot = p * nd + d
    edge = math.isqrt(nt)
    tz, ty = t // edge, lax.rem(t, edge)
    tokens = nd * tg
    mine = tg // 2
    pair = edge // 2

    def rcopy(src, dst, ssem, rsem, to):
        return pltpu.make_async_remote_copy(
            src_ref=src,
            dst_ref=dst,
            send_sem=ssem,
            recv_sem=rsem,
            device_id=to,
            device_id_type=pl.DeviceIdType.MESH,
        )

    others = []
    for a, b in far_first(edge):
        others.append(lax.rem(tz + a, edge) * edge + lax.rem(ty + b, edge))

    def to_plane(ph, src, dst):
        for i, j in enumerate(others):
            rcopy(src(j), dst(i), tsend.at[ph], trecv.at[ph], (p, d, j)).start()

    def plane_wait(ph, like):
        return rcopy(like, like, tsend.at[ph], trecv.at[ph], (p, d, others[-1]))

    def total(first, recv):
        acc = first.astype(F32)
        for i in range(nt - 1):
            acc = acc + recv[i].astype(F32)
        return acc

    def piece(i, g):
        return (g // pair) * edge + i * pair + g % pair

    def side(j):
        return lax.rem(j, edge) // pair

    def unit_group(j):
        return (j // edge) * pair + lax.rem(lax.rem(j, edge), pair)

    my_side = side(t)

    def split(buf, y):
        for i in range(2):
            for g in range(nt // 2):
                blk = y[i * own : (i + 1) * own, g * span : (g + 1) * span]
                buf[piece(i, g), :own] = blk.astype(buf.dtype)

    def side_of(buf, i):
        return jnp.concatenate([buf[piece(i, g), :own] for g in range(nt // 2)], axis=1)

    def join(buf):
        return jnp.concatenate([side_of(buf, 0), side_of(buf, 1)], axis=0)

    def like(buf):
        return buf.at[pl.ds(0, nt - 1)]

    def rs_start(ph, buf, recv):
        to_plane(ph, lambda j: buf.at[j], lambda i: recv.at[i])

    def rs_total(ph, buf, recv):
        plane_wait(ph, recv).wait_recv()
        return total(buf[t], recv)

    def ag_start(ph, buf):
        to_plane(ph, lambda j: buf.at[t], lambda i: buf.at[t])

    def ag_wait(ph, buf):
        plane_wait(ph, like(buf)).wait_recv()

    def ring(k):
        return lax.rem(d + k, nd)

    partner = (1 - p, d, t)

    def to_ring(ph, src, dst):
        for k in (2, 1, 3):
            rcopy(src(ring(k)), dst(ring(k)), xsend.at[ph], xrecv_sem.at[ph], (p, ring(k), t)).start()

    def ring_wait(ph, like):
        return rcopy(like, like, xsend.at[ph], xrecv_sem.at[ph], (p, ring(1), t))

    loads = [
        pltpu.make_async_copy(src, dst, insem.at[i])
        for i, (src, dst) in enumerate(
            (
                (r_hbm, r_ref),
                (u_hbm, u_ref),
                (o_hbm, o_ref),
                (m_hbm, m_ref),
                (v_hbm, v_ref),
                (e_hbm, e_ref),
            )
        )
    ]
    loads[0].start()

    bar = pltpu.get_barrier_semaphore()

    def greet(to):
        pl.semaphore_signal(bar, inc=1, device_id=to, device_id_type=pl.DeviceIdType.MESH)

    for j in others:
        greet((p, d, j))
    for k in range(1, nd):
        greet((p, ring(k), t))
        greet((1 - p, ring(k), t))
    greet(partner)

    loads[0].wait()
    for load in loads[1:]:
        load.start()
    rg[pl.ds(d, 1)] = (r_ref[...] * (1.0 / math.sqrt(width))).astype(BF)[None]
    pl.semaphore_wait(bar, nt - 1 + 2 * (nd - 1) + 1)

    hrow = rows // 2

    def r_half(s, h, to, i):
        blk = rg.at[s, pl.ds(h * hrow, hrow)]
        return rcopy(blk, blk, rsend.at[i], rrecv.at[i], (p, ring(to), t))

    ahead, behind = 1, nd - 1
    r_sends = [
        r_half(d, 0, ahead, 0),
        r_half(d, 1, behind, 1),
        r_half(d, 1, ahead, 2),
        r_half(d, 0, behind, 3),
    ]
    r_gets = [
        r_half(ring(behind), 0, ahead, 0),
        r_half(ring(ahead), 1, behind, 1),
        r_half(ring(behind), 1, ahead, 2),
        r_half(ring(ahead), 0, behind, 3),
    ]
    r_on = [r_half(ring(behind), 0, ahead, 4), r_half(ring(ahead), 1, behind, 5)]
    r_far = [r_half(ring(2), 0, ahead, 4), r_half(ring(2), 1, behind, 5)]
    for c in r_sends:
        c.start()
    for load in loads[1:]:
        load.wait()

    v1_copy = rcopy(v_ref.at[0], v1, psend.at[0], precv.at[0], partner)
    b1_copy = rcopy(bnd, bnd1, psend.at[1], precv.at[1], partner)
    d1_copy = rcopy(dcbuf, dcbuf, psend.at[2], precv.at[2], partner)
    x_copy = rcopy(xpart, xrecv, psend.at[3], precv.at[3], partner)
    xx_copy = rcopy(xgramall.at[0, pl.ds(0, mine)], xx, psend.at[4], precv.at[4], partner)
    g_copy = rcopy(gall.at[d], gall.at[d], psend.at[5], precv.at[5], partner)

    bnd[...] = jnp.broadcast_to(jnp.exp2(m_ref[...].astype(F32)), bnd.shape)

    @pl.when(p == 1)
    def _():
        v1_copy.start()
        split(dcbuf, dot_nt(u_ref[...], o_ref[0]))
        d1_copy.start()
        b1_copy.start()

    @pl.when(p == 0)
    def _():
        split(e2buf, dot_nt(u_ref[...], o_ref[0]))
        v1_copy.wait_recv()
        quarter = pbuf.shape[2]
        cross = dot(o_ref[0], v1[:, pl.ds(pl.multiple_of(d * quarter, quarter), quarter)])
        pbuf[...] = cross.astype(BF).reshape(pbuf.shape)
        to_plane(13, lambda j: pbuf.at[unit_group(j)], lambda i: pbrecv.at[i])
        rs_start(5, e2buf, e2recv)
        d1_copy.wait_recv()
        rs_start(0, dcbuf, dc1recv)

    def e_dot(s):
        return dot(e_ref[:, pl.ds(pl.multiple_of(s * rows, LANES), rows)], rg[s])

    r_gets[0].wait_recv()
    r_on[0].start()
    r_gets[1].wait_recv()
    r_on[1].start()
    part = e_dot(d)
    r_gets[2].wait_recv()
    r_gets[3].wait_recv()
    part = part + e_dot(ring(1)) + e_dot(ring(3))
    r_far[0].wait_recv()
    r_far[1].wait_recv()
    part = part + e_dot(ring(2))
    xpart[...] = part.astype(BF)
    x_copy.start()
    x_copy.wait_recv()
    xall[pl.ds(d, 1)] = (up(xpart[...]) + up(xrecv[...])).astype(BF)[None]

    def share_inputs():
        to_ring(0, lambda j: xall.at[d], lambda j: xall.at[d])
        to_ring(
            1,
            lambda j: e_ref.at[:, pl.ds(pl.multiple_of(j * rows, LANES), rows)],
            lambda j: eall.at[d],
        )
        eall[pl.ds(d, 1)] = e_ref[:, pl.ds(pl.multiple_of(d * rows, LANES), rows)][None]

    gcol = tokens // edge

    def gspot(buf, j):
        grow = buf.shape[1] // edge
        return (
            slice(None),
            pl.ds(pl.multiple_of((j // edge) * grow, grow), grow),
            pl.ds(pl.multiple_of(lax.rem(j, edge) * gcol, gcol), gcol),
        )

    def gram_start(ph, buf, recv):
        to_plane(ph, lambda j: buf.at[gspot(buf, j)], lambda i: recv.at[i])

    def gram_turn(ph, buf, recv, full):
        plane_wait(ph, recv).wait_recv()
        full[gspot(full, t)] = total(buf[gspot(buf, t)], recv).astype(BF)
        blk = full.at[gspot(full, t)]
        to_plane(ph + 1, lambda j: blk, lambda i: blk)

    @pl.when(p == 0)
    def _():
        def diagonal():
            shape = (own, LANES)
            return lax.broadcasted_iota(jnp.int32, shape, 0) == lax.broadcasted_iota(jnp.int32, shape, 1)

        def to_row(col):
            return jnp.sum(jnp.where(diagonal(), col, 0.0), axis=0, keepdims=True)

        def to_col(row):
            return jnp.sum(jnp.where(diagonal(), row, 0.0), axis=1, keepdims=True)

        def store_y(y, h):
            split(ybuf, y)
            hf = up(h)
            sq = jnp.sum(hf * hf, axis=1, keepdims=True)
            for i in range(2):
                tile = jnp.broadcast_to(to_row(sq[i * own : (i + 1) * own]), (8, LANES))
                for g in range(nt // 2):
                    ybuf[piece(i, g), own:] = tile

        def pick(b):
            g = unit_group(t)
            out = b[0:1, :span]
            for i in range(1, nt // 2):
                out = jnp.where(g == i, b[0:1, i * span : (i + 1) * span], out)
            return out

        def norm(tot):
            return lax.rsqrt(to_col(tot[own : own + 1]) / width + 1e-05)

        def gate(tot, dc, inv, bound, buf):
            y = tot[:own]
            z = inv * y
            inside = (z >= -8.0 * bound) & (z <= 7.0 * bound)
            q = (inv * jnp.where(inside, dc, 0.0)).astype(BF)
            coef = to_row(inv * inv / width * jnp.sum(up(q) * y, axis=1, keepdims=True))
            hi = up(coef.astype(BF))
            row = lax.broadcasted_iota(jnp.int32, (16, LANES), 0)
            buf[t, :own] = q
            buf[t, own:] = jnp.where(row == 0, hi, jnp.where(row == 1, coef - hi, 0.0)).astype(BF)

        def coef_of(buf, i):
            ext = up(buf[piece(i, 0), own:])
            for g in range(1, nt // 2):
                ext = ext + up(buf[piece(i, g), own:])
            return to_col(jnp.sum(ext, axis=0, keepdims=True))

        def grad_in(buf, w):
            coef = jnp.concatenate([coef_of(buf, 0), coef_of(buf, 1)], axis=0)
            return dot_nt(join(buf), w), coef

        h0 = xall[d]
        store_y(dot(h0, v_ref[0]), h0)
        rs_start(1, ybuf, y0recv)
        share_inputs()
        plane_wait(13, pbrecv).wait_recv()
        pall[pl.ds(d, 1)] = total(pbuf[unit_group(t)], pbrecv).astype(BF)[None]
        to_ring(3, lambda j: pall.at[d], lambda j: pall.at[d])
        tot0 = rs_total(1, ybuf, y0recv)
        inv0 = norm(tot0)
        bound0 = pick(bnd)
        cbuf[t] = jnp.clip(inv0 * tot0[:own], -8.0 * bound0, 7.0 * bound0).astype(BF)
        ag_start(2, cbuf)
        plane_wait(1, like(ybuf)).wait_send()
        dc1 = rs_total(0, dcbuf, dc1recv)
        e2 = rs_total(5, e2buf, e2recv)
        b1_copy.wait_recv()
        bound1 = pick(bnd1)
        ag_wait(2, cbuf)
        h1 = (up(xall[d]) + dot(join(cbuf), o_ref[0])).astype(BF)
        store_y(dot(h1, v1[...]), h1)
        rs_start(3, ybuf, y1recv)
        split(hobuf, dot_nt(h1, o_ref[0]))
        rs_start(14, hobuf, horecv)
        tot1 = rs_total(3, ybuf, y1recv)
        gate(tot1, dc1, norm(tot1), bound1, qbuf)
        mates, rest = [], []
        for a in (2, 1, 3, 0):
            row = lax.rem(tz + a, edge) * edge
            for c in range(pair - 1, -1, -1):
                if a or c:
                    mates.append(row + my_side * pair + lax.rem(ty + c, pair))
                rest.append(row + (1 - my_side) * pair + lax.rem(ty + c, pair))
        for ph, targets in ((4, mates), (15, rest)):
            for j in targets:
                rcopy(qbuf.at[t], qbuf.at[t], tsend.at[ph], trecv.at[ph], (p, d, j)).start()
        q_mates = plane_wait(4, qbuf.at[pl.ds(0, nt // 2 - 1)])
        q_rest = plane_wait(15, qbuf.at[pl.ds(0, nt // 2)])
        ho = rs_total(14, hobuf, horecv)
        p_three = pall.at[pl.ds(0, nd - 1)]
        ring_wait(3, p_three).wait_recv()
        q_mates.wait_recv()
        q1 = side_of(qbuf, my_side)
        quarter = pall.shape[2]
        dc0 = e2 - coef_of(qbuf, my_side) * ho
        for i in range(nd):
            dc0 = dc0 + dot_nt(q1[:, i * quarter : (i + 1) * quarter], pall[i])
        gate(tot0, dc0, inv0, bound0, q0buf)
        ag_start(6, q0buf)
        q_rest.wait_recv()
        lin, coef = grad_in(qbuf, v1[...])
        u1 = (up(u_ref[...]) + lin - coef * up(h1)).astype(BF)
        ag_wait(6, q0buf)
        lin, coef = grad_in(q0buf, v_ref[0])
        gall[pl.ds(d, 1)] = (up(u1) + lin - coef * up(xall[d])).astype(BF)[None]
        g_copy.start()
        for i in range(2):
            for k in (2, 1, 3):
                rcopy(gall.at[d], gall.at[d], gsend.at[i], grecv.at[i], (i, ring(k), t)).start()

    @pl.when(p == 1)
    def _():
        share_inputs()
        ring_wait(0, xall.at[pl.ds(0, nd - 1)]).wait_recv()
        pair = pl.ds(pl.multiple_of(lax.rem(d, 2) * mine, mine), mine)
        both = jnp.concatenate([xall[i * (nd // 2) + d // 2, pair] for i in range(2)], axis=0)
        xgram[0] = dot_nt(both, xall[...].reshape(tokens, xall.shape[2])).astype(BF)
        gram_start(10, xgram, xgramrecv)
        gram_turn(10, xgram, xgramrecv, xgramall)
        plane_wait(11, xgramrecv).wait_recv()
        xx[...] = xgramall[0, pl.ds(mine, mine)]
        xx_copy.start()
        g_copy.wait_recv()

    vsum = dot_nt(rg[...].reshape(nd * rows, rg.shape[2]), gall[d]).astype(BF)
    vpart[...] = vsum.reshape(nd, rows, tg)
    vrow = rows // nt

    def vspot(j):
        return pl.ds(pl.multiple_of(j * vrow, vrow), vrow)

    to_plane(7, lambda j: vpart.at[:, vspot(j)], lambda i: vrecv.at[i])

    my_group = p * (nd // 2) + d // 2
    my_rows = pl.ds(pl.multiple_of(lax.rem(d, 2) * mine, mine), mine)
    g_three = gall.at[pl.ds(0, nd - 1)]

    @pl.when(p == 0)
    def _():
        ring_wait(0, xall.at[pl.ds(0, nd - 1)]).wait_recv()
        rcopy(g_three, g_three, gsend.at[0], grecv.at[0], partner).wait_recv()

    @pl.when(p == 1)
    def _():
        rcopy(g_three, g_three, gsend.at[1], grecv.at[1], partner).wait_recv()

    hid = xall[...].reshape(tokens, xall.shape[2])
    g_mine = gall[my_group, my_rows]
    x_mine = xall[my_group, my_rows]
    grad = gall[...].reshape(tokens, gall.shape[2])
    gram[0] = dot_nt(g_mine, hid).astype(BF)
    gram[1] = dot_nt(g_mine, grad).astype(BF)
    gram[2] = dot_nt(x_mine, grad).astype(BF)
    gram_start(8, gram, gramrecv)

    plane_wait(7, vrecv).wait_recv()
    vown[...] = total(vpart[:, vspot(t)], vrecv).astype(BF)
    vmine = (tz, ty, slice(None), pl.ds(pl.multiple_of(d * tg, tg), tg))

    def v_turn(step):
        cut = tokens // 2
        lo, hi = pl.ds(0, cut), pl.ds(cut, cut)
        if step == 0:
            along_y, along_z = vall.at[tz, ty, :, lo], vall.at[tz, ty, :, hi]
        else:
            along_y, along_z = vall.at[:, ty, :, hi], vall.at[tz, :, :, lo]
        for k in (2, 1, 3):
            to_y = (p, d, tz * edge + lax.rem(ty + k, edge))
            to_z = (p, d, lax.rem(tz + k, edge) * edge + ty)
            rcopy(along_y, along_y, vasend.at[step, 0], varecv.at[step, 0], to_y).start()
            rcopy(along_z, along_z, vasend.at[step, 1], varecv.at[step, 1], to_z).start()

    def v_waits(step):
        one = pl.ds(0, tokens // 2)
        blk = vall.at[0, pl.ds(0, edge - 1), :, one] if step == 0 else vall.at[pl.ds(0, edge - 1), :, :, one]
        return [rcopy(blk, blk, vasend.at[step, i], varecv.at[step, i], partner) for i in range(2)]

    to_ring(2, lambda j: vown.at[j], lambda j: vall.at[vmine])
    vall[vmine] = vown[d]

    gram_turn(8, gram, gramrecv, gramall)
    v_three = vown.at[pl.ds(0, nd - 1)]
    ring_wait(2, v_three).wait_recv()
    v_turn(0)

    e_three = eall.at[pl.ds(0, nd - 1)]
    ring_wait(1, e_three).wait_recv()
    embt[...] = eall[...].reshape(tokens, rows).T

    @pl.when(p == 0)
    def _():
        xx_copy.wait_recv()

    for c in v_waits(0):
        c.wait_recv()
    v_turn(1)
    plane_wait(9, gramrecv).wait_recv()
    g_x, g_g, x_g, x_x = gramall[0], gramall[1], gramall[2], xx[...]

    def to_group(ph, src, dst):
        for k in (6, 2, 5, 7, 1, 3, 4):
            j = lax.rem(slot + k, group)
            rcopy(src, dst(k), gsend.at[ph], grecv.at[ph], (j // nd, lax.rem(j, nd), t)).start()

    def group_wait(ph, like):
        return rcopy(like, like, gsend.at[ph], grecv.at[ph], partner)

    nsbuf[...] = jnp.broadcast_to(8.0 * jnp.sum(up(x_x) * up(g_g) - up(g_x) * up(x_g)), nsbuf.shape)
    to_group(2, nsbuf, lambda k: nsrecv.at[k - 1])
    place = slot

    def y_ring(k, to):
        blk = yall.at[p * nd + lax.rem(d + to, nd)]
        return rcopy(blk, blk, ysend.at[k], yrecv.at[k], (p, ring(k), t))

    def y_chip(i):
        blk = yall.at[i]
        return rcopy(blk, blk, ysend.at[0], yrecv.at[0], partner)

    yall[place, 0] = (2.0 * (dot(g_x, grad) - dot(g_g, hid))).astype(BF)
    yall[place, 1] = (2.0 * (dot(x_g, hid) - dot(x_x, grad))).astype(BF)
    for k in (2, 1, 3):
        y_ring(k, 0).start()
    y_chip(place).start()


    def vt_of(lanes):
        return vall[:, :, :, lanes].reshape(rows, tokens // 2)

    group_wait(2, nsrecv).wait_recv()
    ns = nsbuf[...]
    for k in range(group - 1):
        ns = ns + nsrecv[k]
    rate = jnp.sqrt(width / (ns[0:1, 0:1] + 1e-06))
    scale = math.sqrt(width)
    for k in (1, 3, 2):
        y_ring(k, nd - k).wait_recv()
        y_chip(p * nd + lax.rem(d + nd - k, nd)).start()
    for c in v_waits(1):
        c.wait_recv()
    y_like = yall.at[pl.ds(0, nd)]
    y_all = rcopy(y_like, y_like, ysend.at[0], yrecv.at[0], partner)

    cut = tokens // 2

    def part_of(i):
        pieces = yall[pl.ds(i * nd, nd)]
        groups = pl.ds(i * (nd // 2), nd // 2)
        za = 2.0 * up(gall[groups].reshape(cut, -1)) - 0.5 * rate * up(pieces[:, 0].reshape(cut, -1))
        zb = -2.0 * up(xall[groups].reshape(cut, -1)) - 0.5 * rate * up(pieces[:, 1].reshape(cut, -1))
        lanes = pl.ds(pl.multiple_of(i * cut, cut), cut)
        return dot(embt[:, lanes], za.astype(BF)) + dot(vt_of(lanes), zb.astype(BF))

    out_ref[...] = r_ref[...] - (0.5 * scale) * rate * part_of(p)
    y_all.wait_recv()
    out_ref[...] = out_ref[...] - (0.5 * scale) * rate * part_of(1 - p)

    for c in r_sends + r_on:
        c.wait_send()
    x_copy.wait_send()
    ring_wait(0, xall.at[pl.ds(0, nd - 1)]).wait_send()
    ring_wait(1, e_three).wait_send()
    ring_wait(2, v_three).wait_send()

    @pl.when(p == 0)
    def _():
        plane_wait(0, like(dcbuf)).wait_send()
        plane_wait(2, like(cbuf)).wait_send()
        plane_wait(3, like(ybuf)).wait_send()
        plane_wait(4, qbuf.at[pl.ds(0, nt // 2 - 1)]).wait_send()
        plane_wait(15, qbuf.at[pl.ds(0, nt // 2)]).wait_send()
        plane_wait(5, like(e2buf)).wait_send()
        plane_wait(6, like(q0buf)).wait_send()
        plane_wait(13, pbrecv).wait_send()
        plane_wait(14, like(hobuf)).wait_send()
        ring_wait(3, pall.at[pl.ds(0, nd - 1)]).wait_send()
        g_copy.wait_send()
        rcopy(g_three, g_three, gsend.at[0], grecv.at[0], partner).wait_send()
        rcopy(g_three, g_three, gsend.at[1], grecv.at[1], partner).wait_send()

    @pl.when(p == 1)
    def _():
        d1_copy.wait_send()
        b1_copy.wait_send()
        v1_copy.wait_send()
        plane_wait(10, xgramrecv).wait_send()
        plane_wait(11, xgramrecv).wait_send()
        xx_copy.wait_send()

    plane_wait(7, vrecv).wait_send()
    plane_wait(8, gramrecv).wait_send()
    plane_wait(9, gramrecv).wait_send()
    for step in range(2):
        for c in v_waits(step):
            c.wait_send()
    group_wait(2, nsrecv).wait_send()
    for k in (1, 2, 3):
        y_ring(k, 0).wait_send()
    y_all.wait_send()


def solution(mesh):
    nd = mesh.shape["dp"]
    nt = mesh.shape["tensor"]

    def local(embedded, rotation, value_proj, output_proj, mid_exponent, cotangent):
        tg = embedded.shape[0]
        rows, cols = rotation.shape
        width = cols * nt
        units = value_proj.shape[2]
        own = tg // 2
        span = units // (nt // 2)
        group = 2 * nd
        edge = math.isqrt(nt)
        mine = tg // 2
        tokens = nd * tg
        vm = pltpu.VMEM
        dma = pltpu.SemaphoreType.DMA
        scratch = [
            vm(embedded.shape, BF),
            vm(rotation.shape, F32),
            vm(value_proj.shape, BF),
            vm(output_proj.shape, BF),
            vm(mid_exponent.shape, jnp.int32),
            vm(cotangent.shape, BF),
            vm((nd, rows, cols), BF),
            vm((tg, cols), BF),
            vm((tg, cols), BF),
            vm((nd, tg, cols), BF),
            vm((nd, tg, rows), BF),
            vm((nd, tg, cols), BF),
            vm((cols, units), BF),
            vm((8, units), F32),
            vm((8, units), F32),
            vm((nt, own, span), BF),
            vm((nt - 1, own, span), BF),
            vm((nt, own, span), BF),
            vm((nt - 1, own, span), BF),
            vm((nt, own, span), BF),
            vm((nt - 1, own, span), BF),
            vm((nt // 2, span, units // nd), BF),
            vm((nt - 1, span, units // nd), BF),
            vm((nd, span, units // nd), BF),
            vm((nt, own + 8, span), YT),
            vm((nt - 1, own + 8, span), YT),
            vm((nt - 1, own + 8, span), YT),
            vm((nt, own, span), BF),
            vm((nt, own + 16, span), BF),
            vm((nt, own + 16, span), BF),
            vm((nd, rows, tg), BF),
            vm((nt - 1, nd, rows // nt, tg), BF),
            vm((nd, rows // nt, tg), BF),
            vm((edge, edge, rows // nt, tokens), BF),
            vm((3, mine, tokens), BF),
            vm((nt - 1, 3, mine // edge, tokens // edge), BF),
            vm((3, mine, tokens), BF),
            vm((1, tg, tokens), BF),
            vm((nt - 1, 1, tg // edge, tokens // edge), BF),
            vm((1, tg, tokens), BF),
            vm((mine, tokens), BF),
            vm((group, 2, mine, cols), BF),
            vm((8, LANES), F32),
            vm((group - 1, 8, LANES), F32),
            vm((rows, tokens), BF),
            dma((6,)),
            dma((16,)),
            dma((16,)),
            dma((12,)),
            dma((12,)),
            dma((4,)),
            dma((4,)),
            dma((3,)),
            dma((3,)),
            dma((6,)),
            dma((6,)),
            dma((nd,)),
            dma((nd,)),
            dma((2, 2)),
            dma((2, 2)),
        ]
        step = pl.pallas_call(
            functools.partial(kernel, nd, nt, float(width)),
            out_shape=pltpu.VMEM((rows, cols), OT),
            in_specs=[pl.BlockSpec(memory_space=pltpu.HBM)] * 6,
            out_specs=pl.BlockSpec(memory_space=pltpu.VMEM),
            scratch_shapes=scratch,
            compiler_params=pltpu.CompilerParams(
                collective_id=0, has_side_effects=True, vmem_limit_bytes=60000000
            ),
        )(*[pltpu.with_memory_space_constraint(x, pltpu.HBM) for x in (embedded, rotation, value_proj, output_proj, mid_exponent, cotangent)])
        return step

    return jax.shard_map(
        local,
        mesh=mesh,
        in_specs=(
            P("dp", "pipe"),
            P(("pipe", "dp"), "tensor"),
            P("pipe", "tensor", None),
            P("pipe", None, "tensor"),
            P("pipe", None),
            P("dp", "tensor"),
        ),
        out_specs=P(("pipe", "dp"), "tensor"),
        check_vma=False,
    )
```

```python
import functools
import math

import jax
import jax.numpy as jnp
from jax import lax
from jax.experimental import pallas as pl
from jax.experimental.pallas import tpu as pltpu
from jax.sharding import PartitionSpec as P

BF = jnp.bfloat16
F32 = jnp.float32
YT = jnp.float32
OT = jnp.float32
LANES = 128
NT_DIMS = (((1,), (1,)), ((), ()))


def dot(a, b):
    return jnp.dot(a, b, preferred_element_type=F32)


def dot_nt(a, b):
    return lax.dot_general(a, b, NT_DIMS, preferred_element_type=F32)


def up(a):
    return a.astype(F32)


def far_first(edge):
    cells = [(a, b) for a in range(edge) for b in range(edge) if a or b]
    hops = [[min(x, edge - x) for x in c] for c in cells]
    return [c for _, c in sorted(zip(hops, cells), key=lambda h: (-sum(h[0]), -h[0][0] if sum(h[0]) > 1 else h[0][0]))]


def kernel(
    nd,
    nt,
    width,
    e_hbm,
    r_hbm,
    v_hbm,
    o_hbm,
    m_hbm,
    u_hbm,
    out_ref,
    e_ref,
    r_ref,
    v_ref,
    o_ref,
    m_ref,
    u_ref,
    rg,
    xpart,
    xrecv,
    xall,
    eall,
    gall,
    v1,
    bnd,
    bnd1,
    dcbuf,
    dc1recv,
    e2buf,
    e2recv,
    hobuf,
    horecv,
    pbuf,
    pbrecv,
    pall,
    ybuf,
    y0recv,
    y1recv,
    cbuf,
    qbuf,
    q0buf,
    vpart,
    vrecv,
    vown,
    vall,
    gram,
    gramrecv,
    gramall,
    eebuf,
    eerecv,
    yall,
    nsbuf,
    nsrecv,
    embt,
    insem,
    tsend,
    trecv,
    rsend,
    rrecv,
    xsend,
    xrecv_sem,
    gsend,
    grecv,
    psend,
    precv,
    ysend,
    yrecv,
    vasend,
    varecv,
):
    p = lax.axis_index("pipe")
    d = lax.axis_index("dp")
    t = lax.axis_index("tensor")
    tg = u_ref.shape[0]
    span = ybuf.shape[2]
    own = tg // 2
    rows = rg.shape[1]
    group = 2 * nd
    slot = p * nd + d
    edge = math.isqrt(nt)
    tz, ty = t // edge, lax.rem(t, edge)
    tokens = nd * tg
    mine = tg // 2
    pair = edge // 2

    def rcopy(src, dst, ssem, rsem, to):
        return pltpu.make_async_remote_copy(
            src_ref=src,
            dst_ref=dst,
            send_sem=ssem,
            recv_sem=rsem,
            device_id=to,
            device_id_type=pl.DeviceIdType.MESH,
        )

    others = []
    for a, b in far_first(edge):
        others.append(lax.rem(tz + a, edge) * edge + lax.rem(ty + b, edge))

    def to_plane(ph, src, dst):
        for i, j in enumerate(others):
            rcopy(src(j), dst(i), tsend.at[ph], trecv.at[ph], (p, d, j)).start()

    def plane_wait(ph, like):
        return rcopy(like, like, tsend.at[ph], trecv.at[ph], (p, d, others[-1]))

    def total(first, recv):
        acc = first.astype(F32)
        for i in range(nt - 1):
            acc = acc + recv[i].astype(F32)
        return acc

    def piece(i, g):
        return (g // pair) * edge + i * pair + g % pair

    def side(j):
        return lax.rem(j, edge) // pair

    def unit_group(j):
        return (j // edge) * pair + lax.rem(lax.rem(j, edge), pair)

    my_side = side(t)

    def split(buf, y):
        for i in range(2):
            for g in range(nt // 2):
                blk = y[i * own : (i + 1) * own, g * span : (g + 1) * span]
                buf[piece(i, g), :own] = blk.astype(buf.dtype)

    def side_of(buf, i):
        return jnp.concatenate([buf[piece(i, g), :own] for g in range(nt // 2)], axis=1)

    def join(buf):
        return jnp.concatenate([side_of(buf, 0), side_of(buf, 1)], axis=0)

    def like(buf):
        return buf.at[pl.ds(0, nt - 1)]

    def rs_start(ph, buf, recv):
        to_plane(ph, lambda j: buf.at[j], lambda i: recv.at[i])

    def rs_total(ph, buf, recv):
        plane_wait(ph, recv).wait_recv()
        return total(buf[t], recv)

    def ag_start(ph, buf):
        to_plane(ph, lambda j: buf.at[t], lambda i: buf.at[t])

    def ag_wait(ph, buf):
        plane_wait(ph, like(buf)).wait_recv()

    def ring(k):
        return lax.rem(d + k, nd)

    partner = (1 - p, d, t)

    def to_ring(ph, src, dst):
        for k in (2, 1, 3):
            rcopy(src(ring(k)), dst(ring(k)), xsend.at[ph], xrecv_sem.at[ph], (p, ring(k), t)).start()

    def ring_wait(ph, like):
        return rcopy(like, like, xsend.at[ph], xrecv_sem.at[ph], (p, ring(1), t))

    loads = [
        pltpu.make_async_copy(src, dst, insem.at[i])
        for i, (src, dst) in enumerate(
            (
                (r_hbm, r_ref),
                (u_hbm, u_ref),
                (o_hbm, o_ref),
                (m_hbm, m_ref),
                (v_hbm, v_ref),
                (e_hbm, e_ref),
            )
        )
    ]
    loads[0].start()

    bar = pltpu.get_barrier_semaphore()

    def greet(to):
        pl.semaphore_signal(bar, inc=1, device_id=to, device_id_type=pl.DeviceIdType.MESH)

    for j in others:
        greet((p, d, j))
    for k in range(1, nd):
        greet((p, ring(k), t))
        greet((1 - p, ring(k), t))
    greet(partner)

    loads[0].wait()
    for load in loads[1:]:
        load.start()
    rg[pl.ds(d, 1)] = (r_ref[...] * (1.0 / math.sqrt(width))).astype(BF)[None]
    pl.semaphore_wait(bar, nt - 1 + 2 * (nd - 1) + 1)

    hrow = rows // 2

    def r_half(s, h, to, i):
        blk = rg.at[s, pl.ds(h * hrow, hrow)]
        return rcopy(blk, blk, rsend.at[i], rrecv.at[i], (p, ring(to), t))

    ahead, behind = 1, nd - 1
    r_sends = [
        r_half(d, 0, ahead, 0),
        r_half(d, 1, behind, 1),
        r_half(d, 1, ahead, 2),
        r_half(d, 0, behind, 3),
    ]
    r_gets = [
        r_half(ring(behind), 0, ahead, 0),
        r_half(ring(ahead), 1, behind, 1),
        r_half(ring(behind), 1, ahead, 2),
        r_half(ring(ahead), 0, behind, 3),
    ]
    r_on = [r_half(ring(behind), 0, ahead, 4), r_half(ring(ahead), 1, behind, 5)]
    r_far = [r_half(ring(2), 0, ahead, 4), r_half(ring(2), 1, behind, 5)]
    for c in r_sends:
        c.start()
    for load in loads[1:]:
        load.wait()

    v1_copy = rcopy(v_ref.at[0], v1, psend.at[0], precv.at[0], partner)
    b1_copy = rcopy(bnd, bnd1, psend.at[1], precv.at[1], partner)
    d1_copy = rcopy(dcbuf, dcbuf, psend.at[2], precv.at[2], partner)
    x_copy = rcopy(xpart, xrecv, psend.at[3], precv.at[3], partner)
    g_copy = rcopy(gall.at[d], gall.at[d], psend.at[5], precv.at[5], partner)

    bnd[...] = jnp.broadcast_to(jnp.exp2(m_ref[...].astype(F32)), bnd.shape)

    @pl.when(p == 1)
    def _():
        v1_copy.start()
        split(dcbuf, dot_nt(u_ref[...], o_ref[0]))
        d1_copy.start()
        b1_copy.start()

    @pl.when(p == 0)
    def _():
        split(e2buf, dot_nt(u_ref[...], o_ref[0]))
        v1_copy.wait_recv()
        quarter = pbuf.shape[2]
        cross = dot(o_ref[0], v1[:, pl.ds(pl.multiple_of(d * quarter, quarter), quarter)])
        pbuf[...] = cross.astype(BF).reshape(pbuf.shape)
        to_plane(13, lambda j: pbuf.at[unit_group(j)], lambda i: pbrecv.at[i])
        rs_start(5, e2buf, e2recv)
        d1_copy.wait_recv()
        rs_start(0, dcbuf, dc1recv)

    def e_dot(s):
        return dot(e_ref[:, pl.ds(pl.multiple_of(s * rows, LANES), rows)], rg[s])

    r_gets[0].wait_recv()
    r_on[0].start()
    r_gets[1].wait_recv()
    r_on[1].start()
    part = e_dot(d)
    r_gets[2].wait_recv()
    r_gets[3].wait_recv()
    part = part + e_dot(ring(1)) + e_dot(ring(3))
    r_far[0].wait_recv()
    r_far[1].wait_recv()
    part = part + e_dot(ring(2))
    xpart[...] = part.astype(BF)
    x_copy.start()
    x_copy.wait_recv()
    xall[pl.ds(d, 1)] = (up(xpart[...]) + up(xrecv[...])).astype(BF)[None]

    def to_group(ph, src, dst):
        for k in (6, 2, 5, 7, 1, 3, 4):
            j = lax.rem(slot + k, group)
            rcopy(src(j), dst(k), gsend.at[ph], grecv.at[ph], (j // nd, lax.rem(j, nd), t)).start()

    def group_wait(ph, like):
        return rcopy(like, like, gsend.at[ph], grecv.at[ph], partner)

    e_three = eall.at[pl.ds(0, nd - 1)]

    def share_gram():
        ring_wait(1, e_three).wait_recv()
        emb = eall[...].reshape(tokens, rows)
        eebuf[...] = dot_nt(emb, emb).astype(BF).reshape(eebuf.shape)
        to_group(3, lambda j: eebuf.at[j], lambda k: eerecv.at[k - 1])

    def share_inputs():
        to_ring(0, lambda j: xall.at[d], lambda j: xall.at[d])
        to_ring(
            1,
            lambda j: e_ref.at[:, pl.ds(pl.multiple_of(j * rows, LANES), rows)],
            lambda j: eall.at[d],
        )
        eall[pl.ds(d, 1)] = e_ref[:, pl.ds(pl.multiple_of(d * rows, LANES), rows)][None]

    gcol = tokens // edge

    def gspot(buf, j):
        grow = buf.shape[1] // edge
        return (
            slice(None),
            pl.ds(pl.multiple_of((j // edge) * grow, grow), grow),
            pl.ds(pl.multiple_of(lax.rem(j, edge) * gcol, gcol), gcol),
        )

    def gram_start(ph, buf, recv):
        to_plane(ph, lambda j: buf.at[gspot(buf, j)], lambda i: recv.at[i])

    def gram_turn(ph, buf, recv, full):
        plane_wait(ph, recv).wait_recv()
        full[gspot(full, t)] = total(buf[gspot(buf, t)], recv).astype(BF)
        blk = full.at[gspot(full, t)]
        to_plane(ph + 1, lambda j: blk, lambda i: blk)

    @pl.when(p == 0)
    def _():
        def diagonal():
            shape = (own, LANES)
            return lax.broadcasted_iota(jnp.int32, shape, 0) == lax.broadcasted_iota(jnp.int32, shape, 1)

        def to_row(col):
            return jnp.sum(jnp.where(diagonal(), col, 0.0), axis=0, keepdims=True)

        def to_col(row):
            return jnp.sum(jnp.where(diagonal(), row, 0.0), axis=1, keepdims=True)

        def store_y(y, h):
            split(ybuf, y)
            hf = up(h)
            sq = jnp.sum(hf * hf, axis=1, keepdims=True)
            for i in range(2):
                tile = jnp.broadcast_to(to_row(sq[i * own : (i + 1) * own]), (8, LANES))
                for g in range(nt // 2):
                    ybuf[piece(i, g), own:] = tile

        def pick(b):
            g = unit_group(t)
            out = b[0:1, :span]
            for i in range(1, nt // 2):
                out = jnp.where(g == i, b[0:1, i * span : (i + 1) * span], out)
            return out

        def norm(tot):
            return lax.rsqrt(to_col(tot[own : own + 1]) / width + 1e-05)

        def gate(tot, dc, inv, bound, buf):
            y = tot[:own]
            z = inv * y
            inside = (z >= -8.0 * bound) & (z <= 7.0 * bound)
            q = (inv * jnp.where(inside, dc, 0.0)).astype(BF)
            coef = to_row(inv * inv / width * jnp.sum(up(q) * y, axis=1, keepdims=True))
            hi = up(coef.astype(BF))
            row = lax.broadcasted_iota(jnp.int32, (16, LANES), 0)
            buf[t, :own] = q
            buf[t, own:] = jnp.where(row == 0, hi, jnp.where(row == 1, coef - hi, 0.0)).astype(BF)

        def coef_of(buf, i):
            ext = up(buf[piece(i, 0), own:])
            for g in range(1, nt // 2):
                ext = ext + up(buf[piece(i, g), own:])
            return to_col(jnp.sum(ext, axis=0, keepdims=True))

        def grad_in(buf, w):
            coef = jnp.concatenate([coef_of(buf, 0), coef_of(buf, 1)], axis=0)
            return dot_nt(join(buf), w), coef

        h0 = xall[d]
        store_y(dot(h0, v_ref[0]), h0)
        rs_start(1, ybuf, y0recv)
        share_inputs()
        plane_wait(13, pbrecv).wait_recv()
        pall[pl.ds(d, 1)] = total(pbuf[unit_group(t)], pbrecv).astype(BF)[None]
        to_ring(3, lambda j: pall.at[d], lambda j: pall.at[d])
        tot0 = rs_total(1, ybuf, y0recv)
        inv0 = norm(tot0)
        bound0 = pick(bnd)
        cbuf[t] = jnp.clip(inv0 * tot0[:own], -8.0 * bound0, 7.0 * bound0).astype(BF)
        ag_start(2, cbuf)
        plane_wait(1, like(ybuf)).wait_send()
        dc1 = rs_total(0, dcbuf, dc1recv)
        e2 = rs_total(5, e2buf, e2recv)
        b1_copy.wait_recv()
        bound1 = pick(bnd1)
        ag_wait(2, cbuf)
        h1 = (up(xall[d]) + dot(join(cbuf), o_ref[0])).astype(BF)
        store_y(dot(h1, v1[...]), h1)
        rs_start(3, ybuf, y1recv)
        split(hobuf, dot_nt(h1, o_ref[0]))
        rs_start(14, hobuf, horecv)
        tot1 = rs_total(3, ybuf, y1recv)
        gate(tot1, dc1, norm(tot1), bound1, qbuf)
        mates, rest = [], []
        for a in (2, 1, 3, 0):
            row = lax.rem(tz + a, edge) * edge
            for c in range(pair - 1, -1, -1):
                if a or c:
                    mates.append(row + my_side * pair + lax.rem(ty + c, pair))
                rest.append(row + (1 - my_side) * pair + lax.rem(ty + c, pair))
        for ph, targets in ((4, mates), (15, rest)):
            for j in targets:
                rcopy(qbuf.at[t], qbuf.at[t], tsend.at[ph], trecv.at[ph], (p, d, j)).start()
        q_mates = plane_wait(4, qbuf.at[pl.ds(0, nt // 2 - 1)])
        q_rest = plane_wait(15, qbuf.at[pl.ds(0, nt // 2)])
        share_gram()
        ho = rs_total(14, hobuf, horecv)
        p_three = pall.at[pl.ds(0, nd - 1)]
        ring_wait(3, p_three).wait_recv()
        q_mates.wait_recv()
        q1 = side_of(qbuf, my_side)
        quarter = pall.shape[2]
        dc0 = e2 - coef_of(qbuf, my_side) * ho
        for i in range(nd):
            dc0 = dc0 + dot_nt(q1[:, i * quarter : (i + 1) * quarter], pall[i])
        gate(tot0, dc0, inv0, bound0, q0buf)
        ag_start(6, q0buf)
        q_rest.wait_recv()
        lin, coef = grad_in(qbuf, v1[...])
        u1 = (up(u_ref[...]) + lin - coef * up(h1)).astype(BF)
        ag_wait(6, q0buf)
        lin, coef = grad_in(q0buf, v_ref[0])
        gall[pl.ds(d, 1)] = (up(u1) + lin - coef * up(xall[d])).astype(BF)[None]
        g_copy.start()
        for i in range(2):
            for k in (2, 1, 3):
                rcopy(gall.at[d], gall.at[d], gsend.at[i], grecv.at[i], (i, ring(k), t)).start()

    @pl.when(p == 1)
    def _():
        share_inputs()
        share_gram()
        ring_wait(0, xall.at[pl.ds(0, nd - 1)]).wait_recv()
        g_copy.wait_recv()

    vsum = dot_nt(rg[...].reshape(nd * rows, rg.shape[2]), gall[d]).astype(BF)
    vpart[...] = vsum.reshape(nd, rows, tg)
    vrow = rows // nt

    def vspot(j):
        return pl.ds(pl.multiple_of(j * vrow, vrow), vrow)

    to_plane(7, lambda j: vpart.at[:, vspot(j)], lambda i: vrecv.at[i])

    my_group = p * (nd // 2) + d // 2
    my_rows = pl.ds(pl.multiple_of(lax.rem(d, 2) * mine, mine), mine)
    g_three = gall.at[pl.ds(0, nd - 1)]

    @pl.when(p == 0)
    def _():
        ring_wait(0, xall.at[pl.ds(0, nd - 1)]).wait_recv()
        rcopy(g_three, g_three, gsend.at[0], grecv.at[0], partner).wait_recv()

    @pl.when(p == 1)
    def _():
        rcopy(g_three, g_three, gsend.at[1], grecv.at[1], partner).wait_recv()

    hid = xall[...].reshape(tokens, xall.shape[2])
    g_mine = gall[my_group, my_rows]
    x_mine = xall[my_group, my_rows]
    grad = gall[...].reshape(tokens, gall.shape[2])
    gram[0] = dot_nt(g_mine, hid).astype(BF)
    gram[1] = dot_nt(g_mine, grad).astype(BF)
    gram[2] = dot_nt(x_mine, grad).astype(BF)
    gram_start(8, gram, gramrecv)

    plane_wait(7, vrecv).wait_recv()
    vown[...] = total(vpart[:, vspot(t)], vrecv).astype(BF)
    vmine = (tz, ty, slice(None), pl.ds(pl.multiple_of(d * tg, tg), tg))

    def v_turn(step):
        cut = tokens // 2
        lo, hi = pl.ds(0, cut), pl.ds(cut, cut)
        if step == 0:
            along_y, along_z = vall.at[tz, ty, :, lo], vall.at[tz, ty, :, hi]
        else:
            along_y, along_z = vall.at[:, ty, :, hi], vall.at[tz, :, :, lo]
        for k in (2, 1, 3):
            to_y = (p, d, tz * edge + lax.rem(ty + k, edge))
            to_z = (p, d, lax.rem(tz + k, edge) * edge + ty)
            rcopy(along_y, along_y, vasend.at[step, 0], varecv.at[step, 0], to_y).start()
            rcopy(along_z, along_z, vasend.at[step, 1], varecv.at[step, 1], to_z).start()

    def v_waits(step):
        one = pl.ds(0, tokens // 2)
        blk = vall.at[0, pl.ds(0, edge - 1), :, one] if step == 0 else vall.at[pl.ds(0, edge - 1), :, :, one]
        return [rcopy(blk, blk, vasend.at[step, i], varecv.at[step, i], partner) for i in range(2)]

    to_ring(2, lambda j: vown.at[j], lambda j: vall.at[vmine])
    vall[vmine] = vown[d]

    gram_turn(8, gram, gramrecv, gramall)
    v_three = vown.at[pl.ds(0, nd - 1)]
    ring_wait(2, v_three).wait_recv()
    v_turn(0)

    embt[...] = eall[...].reshape(tokens, rows).T

    group_wait(3, eerecv).wait_recv()
    ee = up(eebuf[slot])
    for k in range(group - 1):
        ee = ee + up(eerecv[k])
    x_x = ee.astype(BF)

    for c in v_waits(0):
        c.wait_recv()
    v_turn(1)
    plane_wait(9, gramrecv).wait_recv()
    g_x, g_g, x_g = gramall[0], gramall[1], gramall[2]

    nsbuf[...] = jnp.broadcast_to(8.0 * jnp.sum(up(x_x) * up(g_g) - up(g_x) * up(x_g)), nsbuf.shape)
    to_group(2, lambda j: nsbuf, lambda k: nsrecv.at[k - 1])
    place = slot

    def y_ring(k, to):
        blk = yall.at[p * nd + lax.rem(d + to, nd)]
        return rcopy(blk, blk, ysend.at[k], yrecv.at[k], (p, ring(k), t))

    def y_chip(i):
        blk = yall.at[i]
        return rcopy(blk, blk, ysend.at[0], yrecv.at[0], partner)

    yall[place, 0] = (2.0 * (dot(g_x, grad) - dot(g_g, hid))).astype(BF)
    yall[place, 1] = (2.0 * (dot(x_g, hid) - dot(x_x, grad))).astype(BF)
    for k in (2, 1, 3):
        y_ring(k, 0).start()
    y_chip(place).start()


    def vt_of(lanes):
        return vall[:, :, :, lanes].reshape(rows, tokens // 2)

    group_wait(2, nsrecv).wait_recv()
    ns = nsbuf[...]
    for k in range(group - 1):
        ns = ns + nsrecv[k]
    rate = jnp.sqrt(width / (ns[0:1, 0:1] + 1e-06))
    scale = math.sqrt(width)
    for k in (1, 3, 2):
        y_ring(k, nd - k).wait_recv()
        y_chip(p * nd + lax.rem(d + nd - k, nd)).start()
    for c in v_waits(1):
        c.wait_recv()
    y_like = yall.at[pl.ds(0, nd)]
    y_all = rcopy(y_like, y_like, ysend.at[0], yrecv.at[0], partner)

    cut = tokens // 2

    def part_of(i):
        pieces = yall[pl.ds(i * nd, nd)]
        groups = pl.ds(i * (nd // 2), nd // 2)
        za = 2.0 * up(gall[groups].reshape(cut, -1)) - 0.5 * rate * up(pieces[:, 0].reshape(cut, -1))
        zb = -2.0 * up(xall[groups].reshape(cut, -1)) - 0.5 * rate * up(pieces[:, 1].reshape(cut, -1))
        lanes = pl.ds(pl.multiple_of(i * cut, cut), cut)
        return dot(embt[:, lanes], za.astype(BF)) + dot(vt_of(lanes), zb.astype(BF))

    out_ref[...] = r_ref[...] - (0.5 * scale) * rate * part_of(p)
    y_all.wait_recv()
    out_ref[...] = out_ref[...] - (0.5 * scale) * rate * part_of(1 - p)

    for c in r_sends + r_on:
        c.wait_send()
    x_copy.wait_send()
    ring_wait(0, xall.at[pl.ds(0, nd - 1)]).wait_send()
    ring_wait(1, e_three).wait_send()
    ring_wait(2, v_three).wait_send()

    @pl.when(p == 0)
    def _():
        plane_wait(0, like(dcbuf)).wait_send()
        plane_wait(2, like(cbuf)).wait_send()
        plane_wait(3, like(ybuf)).wait_send()
        plane_wait(4, qbuf.at[pl.ds(0, nt // 2 - 1)]).wait_send()
        plane_wait(15, qbuf.at[pl.ds(0, nt // 2)]).wait_send()
        plane_wait(5, like(e2buf)).wait_send()
        plane_wait(6, like(q0buf)).wait_send()
        plane_wait(13, pbrecv).wait_send()
        plane_wait(14, like(hobuf)).wait_send()
        ring_wait(3, pall.at[pl.ds(0, nd - 1)]).wait_send()
        g_copy.wait_send()
        rcopy(g_three, g_three, gsend.at[0], grecv.at[0], partner).wait_send()
        rcopy(g_three, g_three, gsend.at[1], grecv.at[1], partner).wait_send()

    @pl.when(p == 1)
    def _():
        d1_copy.wait_send()
        b1_copy.wait_send()
        v1_copy.wait_send()

    plane_wait(7, vrecv).wait_send()
    plane_wait(8, gramrecv).wait_send()
    plane_wait(9, gramrecv).wait_send()
    for step in range(2):
        for c in v_waits(step):
            c.wait_send()
    group_wait(2, nsrecv).wait_send()
    group_wait(3, eerecv).wait_send()
    for k in (1, 2, 3):
        y_ring(k, 0).wait_send()
    y_all.wait_send()


def solution(mesh):
    nd = mesh.shape["dp"]
    nt = mesh.shape["tensor"]

    def local(embedded, rotation, value_proj, output_proj, mid_exponent, cotangent):
        tg = embedded.shape[0]
        rows, cols = rotation.shape
        width = cols * nt
        units = value_proj.shape[2]
        own = tg // 2
        span = units // (nt // 2)
        group = 2 * nd
        edge = math.isqrt(nt)
        mine = tg // 2
        tokens = nd * tg
        vm = pltpu.VMEM
        dma = pltpu.SemaphoreType.DMA
        scratch = [
            vm(embedded.shape, BF),
            vm(rotation.shape, F32),
            vm(value_proj.shape, BF),
            vm(output_proj.shape, BF),
            vm(mid_exponent.shape, jnp.int32),
            vm(cotangent.shape, BF),
            vm((nd, rows, cols), BF),
            vm((tg, cols), BF),
            vm((tg, cols), BF),
            vm((nd, tg, cols), BF),
            vm((nd, tg, rows), BF),
            vm((nd, tg, cols), BF),
            vm((cols, units), BF),
            vm((8, units), F32),
            vm((8, units), F32),
            vm((nt, own, span), BF),
            vm((nt - 1, own, span), BF),
            vm((nt, own, span), BF),
            vm((nt - 1, own, span), BF),
            vm((nt, own, span), BF),
            vm((nt - 1, own, span), BF),
            vm((nt // 2, span, units // nd), BF),
            vm((nt - 1, span, units // nd), BF),
            vm((nd, span, units // nd), BF),
            vm((nt, own + 8, span), YT),
            vm((nt - 1, own + 8, span), YT),
            vm((nt - 1, own + 8, span), YT),
            vm((nt, own, span), BF),
            vm((nt, own + 16, span), BF),
            vm((nt, own + 16, span), BF),
            vm((nd, rows, tg), BF),
            vm((nt - 1, nd, rows // nt, tg), BF),
            vm((nd, rows // nt, tg), BF),
            vm((edge, edge, rows // nt, tokens), BF),
            vm((3, mine, tokens), BF),
            vm((nt - 1, 3, mine // edge, tokens // edge), BF),
            vm((3, mine, tokens), BF),
            vm((group, mine, tokens), BF),
            vm((group - 1, mine, tokens), BF),
            vm((group, 2, mine, cols), BF),
            vm((8, LANES), F32),
            vm((group - 1, 8, LANES), F32),
            vm((rows, tokens), BF),
            dma((6,)),
            dma((16,)),
            dma((16,)),
            dma((12,)),
            dma((12,)),
            dma((4,)),
            dma((4,)),
            dma((4,)),
            dma((4,)),
            dma((6,)),
            dma((6,)),
            dma((nd,)),
            dma((nd,)),
            dma((2, 2)),
            dma((2, 2)),
        ]
        step = pl.pallas_call(
            functools.partial(kernel, nd, nt, float(width)),
            out_shape=pltpu.VMEM((rows, cols), OT),
            in_specs=[pl.BlockSpec(memory_space=pltpu.HBM)] * 6,
            out_specs=pl.BlockSpec(memory_space=pltpu.VMEM),
            scratch_shapes=scratch,
            compiler_params=pltpu.CompilerParams(
                collective_id=0, has_side_effects=True, vmem_limit_bytes=60000000
            ),
        )(*[pltpu.with_memory_space_constraint(x, pltpu.HBM) for x in (embedded, rotation, value_proj, output_proj, mid_exponent, cotangent)])
        return step

    return jax.shard_map(
        local,
        mesh=mesh,
        in_specs=(
            P("dp", "pipe"),
            P(("pipe", "dp"), "tensor"),
            P("pipe", "tensor", None),
            P("pipe", None, "tensor"),
            P("pipe", None),
            P("dp", "tensor"),
        ),
        out_specs=P(("pipe", "dp"), "tensor"),
        check_vma=False,
    )
```
